128 devices in a mesh: samp: 16 (over z, y), col: 8 (over x, core).
Axes of the slice: x: 4, y: 4, z: 4, core: 2. Of those that a mesh axis runs over, the one named last changes fastest.
Arguments:
- spectra: float32 [32768, 8192], P('samp', 'col'), as said below
- w_start: float32 [32768, 512], P('samp'), may hold values from 0.05 to 1
- h_start: float32 [8192, 512], P('col'), may hold values from 0.05 to 1
Outputs:
- w_factor: float32 [32768, 512], P('samp')
- h_factor: float32 [8192, 512], P('col')
The draws below stay inside these ranges and needn't reach their ends.
Inputs may be any that keep to these rules, and one draw needn't show every extreme that they name: `spectra`: every entry is positive.
All inputs are finite; a program needn't handle non-finite values.
Results may differ from the reference program's by a relative error of at most 0.0003.
Values sent between devices are 32-bit elements; how exact they have to be, the bound alone decides.
No kernel may reach another device: no remote copies, remote signals or barrier semaphores. Data moves between devices by JAX's collectives and lax.ppermute only.
A program may use at most 128 MiB of HBM per device.

```python
import math
import jax
import jax.numpy as jnp
from jax import lax

K = 512
N = 8192
BLOCK = 128
SWEEPS = 3
M = 32768


def draw_spectra(key, part):
    key_rows, key_cols, key_cells = jax.random.split(key, 3)
    row_scale = jnp.exp(jax.random.uniform(key_rows, (M, 1), jnp.float32, math.log(0.3), math.log(3.0)))
    col_scale = jnp.exp(jax.random.uniform(key_cols, (1, N), jnp.float32, math.log(0.3), math.log(3.0)))
    cells = jnp.exp(jax.random.uniform(key_cells, (M, N), jnp.float32, math.log(0.5), math.log(2.0)))
    return (64.0 * row_scale * col_scale * cells).astype(jnp.float32)


def block_scale(rng, extent, cuts, low, high):
    def one(axis_at, parts):
        draws = jax.random.uniform(jax.random.fold_in(jax.random.fold_in(rng, 6), axis_at), (parts,), jnp.float32, low / len(cuts), high / len(cuts))
        return jnp.repeat(jnp.exp(draws), extent[axis_at] // parts).reshape((-1,) + (1,) * (len(extent) - axis_at - 1))

    loudness = one(*cuts[0])
    for cut in cuts[1:]:
        loudness = loudness * one(*cut)
    return loudness


def setup_inputs(seed: int = 0) -> dict:
    streams_of = jax.random.split(jax.random.key(seed), 4)
    spectra = draw_spectra(jax.random.fold_in(streams_of[3], 71), 0)
    w_start = jnp.clip(0.05 + 0.95 * jax.random.uniform(streams_of[1], (M, K), jnp.float32) ** block_scale(streams_of[1], (M, K), ((0, 16),), -0.2, 0.2), 0.05, 1.0)
    h_start = jnp.clip(0.05 + 0.95 * jax.random.uniform(streams_of[2], (N, K), jnp.float32) ** block_scale(streams_of[2], (N, K), ((0, 8),), -0.2, 0.2), 0.05, 1.0)
    return dict(spectra=spectra, w_start=w_start, h_start=h_start)


floor_value = 1e-6


def sweep_factor(factor, product, gram_matrix):
    rank_width = gram_matrix.shape[0]
    for sweep_index in range(SWEEPS):
        for offset in range(0, rank_width, BLOCK):
            gram_cols = gram_matrix[:, offset:offset + BLOCK]
            majorant = jnp.sum(gram_matrix[offset:offset + BLOCK, offset:offset + BLOCK], axis=1)
            update = product[:, offset:offset + BLOCK] - jnp.dot(factor, gram_cols, precision=lax.Precision.HIGHEST, preferred_element_type=jnp.float32)
            new_block = jnp.maximum(factor[:, offset:offset + BLOCK] + update / majorant, floor_value)
            factor = lax.dynamic_update_slice_in_dim(factor, new_block, offset, 1)
    return factor


def contract_rows(left, right):
    return lax.dot_general(left, right, (((0,), (0,)), ((), ())), precision=lax.Precision.HIGHEST, preferred_element_type=jnp.float32)


def reference(spectra, w_start, h_start):
    prod_w = jnp.dot(spectra, h_start, precision=lax.Precision.HIGHEST, preferred_element_type=jnp.float32)
    gram_h = contract_rows(h_start, h_start)
    w_factor = sweep_factor(w_start, prod_w, gram_h)
    prod_h = contract_rows(spectra, w_factor)
    gram_w = contract_rows(w_factor, w_factor)
    h_factor = sweep_factor(h_start, prod_h, gram_w)
    return w_factor, h_factor
```

```python
import functools
import jax
import jax.numpy as jnp
from jax import lax
from jax.experimental import pallas as pl
from jax.experimental.pallas import tpu as pltpu
from jax.sharding import PartitionSpec as P

BLOCK = 128
SWEEPS = 3
floor_value = 1e-06
REL = (0, 1, 3, 2)
f32, bf16 = jnp.float32, jnp.bfloat16
ANY = pl.BlockSpec(memory_space=pl.ANY)
HBM = pl.BlockSpec(memory_space=pltpu.HBM)
VM = pl.BlockSpec(memory_space=pltpu.VMEM)


def sds(*shape, dtype=f32):
    return jax.ShapeDtypeStruct(shape, dtype)


def cost(flops, nbytes):
    return pl.CostEstimate(flops=flops, bytes_accessed=nbytes, transcendentals=0)


def params(mib):
    return pltpu.CompilerParams(vmem_limit_bytes=mib << 20)


def split(a):
    hi = a.astype(bf16)
    return hi, (a - hi.astype(f32)).astype(bf16)


def dot3(ah, al, bh, bl):
    d = functools.partial(jnp.dot, preferred_element_type=f32)
    return d(ah, bh) + (d(ah, bl) + d(al, bh))


def place():
    s, q = lax.axis_index("samp"), lax.axis_index("col")
    return s // 4, s % 4, q // 2, q % 2


def prod_kernel(chunks, sibling, first, nadd, *refs):
    refs = list(refs)
    x_ref = refs.pop(0)
    if first:
        h_ref = refs.pop(0)
    else:
        hh_ref, hl_ref = refs.pop(0), refs.pop(0)
    adds = [refs.pop(0) for _ in range(nadd)]
    out_ref = refs.pop(0)
    if first:
        hh_ref, hl_ref = refs.pop(0), refs.pop(0)
    xs, sem = refs
    _, _, _, c = place()
    cc = 1 - c if sibling else c
    copies = []
    for i, k in enumerate(chunks):
        row = pl.multiple_of(512 * k + 256 * cc, 256)
        cp = pltpu.make_async_copy(x_ref.at[pl.ds(row, 256), :], xs.at[pl.ds(256 * i, 256), :], sem.at[i])
        cp.start()
        copies.append(cp)
    if first:
        hh, hl = split(h_ref[...])
        hh_ref[...] = hh
        hl_ref[...] = hl
    if nadd:
        n = adds[0].shape[0]
        out_ref[:n, :] = adds[0][...] + adds[1][:n, :]
    else:
        n = 0
    for at in range(0, 256 * len(chunks), 512):
        copies[at // 256].wait()
        copies[at // 256 + 1].wait()
        ah, al = split(xs[at : at + 512, :])
        out = dot3(ah, al, hh_ref[...], hl_ref[...])
        if nadd:
            out = out + adds[1][n + at : n + at + 512, :]
        out_ref[n + at : n + at + 512, :] = out


def prod(spectra, h, chunks, sibling, adds=()):
    first = not isinstance(h, tuple)
    n = 256 * len(chunks)
    ins = [spectra] + ([h] if first else list(h)) + list(adds)
    outs = [sds(n + (adds[0].shape[0] if adds else 0), 512)]
    if first:
        outs += [sds(1024, 512, dtype=bf16)] * 2
    out = pl.pallas_call(
        functools.partial(prod_kernel, chunks, sibling, first, len(adds)),
        out_shape=outs,
        in_specs=[HBM] + [VM] * (len(ins) - 1),
        out_specs=[VM] * len(outs),
        scratch_shapes=[pltpu.VMEM((n, 1024), f32), pltpu.SemaphoreType.DMA((len(chunks),))],
        compiler_params=params(50),
        cost_estimate=cost(6 * n * 1024 * 512, n * 6144 + (2 << 20)),
        name="prod",
    )(*ins)
    return out if first else out[0]


def flip_kernel(x_ref, th_ref, tl_ref):
    for k in range(0, 1024, 128):
        hi, lo = split(x_ref[:, k : k + 128].T)
        th_ref[0, k : k + 128, :] = hi
        tl_ref[0, k : k + 128, :] = lo


def flip(spectra):
    spec = pl.BlockSpec((1, 1024, 128), lambda i: (i, 0, 0))
    return pl.pallas_call(
        flip_kernel,
        grid=(16,),
        out_shape=[sds(16, 1024, 128, dtype=bf16)] * 2,
        in_specs=[pl.BlockSpec((128, 1024), lambda i: (i, 0))],
        out_specs=[spec, spec],
        compiler_params=params(6),
        cost_estimate=cost(1 << 24, 16 << 20),
        name="flip",
    )(spectra)


def back_kernel(chunks, later, *refs):
    refs = list(refs)
    th_ref, tl_ref = refs.pop(0), refs.pop(0)
    ws = [refs.pop(0) for _ in chunks]
    acc_ref = refs.pop(0) if later else None
    if later:
        refs.pop(0)
    out_ref, w_out, sem = refs
    z, y, x, c = place()
    at, copies = [], []
    for k, (r, sibling) in enumerate(chunks):
        first = 2 * (2 * ((x + r) % 4) + (1 - c if sibling else c))
        at += [first, first + 1]
        cp = pltpu.make_async_copy(ws[k], w_out.at[pl.ds(pl.multiple_of(128 * first, 256), 256), :], sem.at[k])
        cp.start()
        copies.append(cp)
    wh, wl = split(jnp.concatenate([w[...] for w in ws], axis=0))
    for k in range(0, 1024, 512):
        rows = slice(k, k + 512)
        ah = jnp.concatenate([th_ref[i, rows, :] for i in at], axis=1)
        al = jnp.concatenate([tl_ref[i, rows, :] for i in at], axis=1)
        out = dot3(ah, al, wh, wl)
        if later:
            out = out + acc_ref[rows, :]
        out_ref[rows, :] = out
    for cp in copies:
        cp.wait()


def back(flipped, ws, chunks, carry=()):
    ins = list(flipped) + list(ws) + list(carry)
    n = len(ins)
    return pl.pallas_call(
        functools.partial(back_kernel, tuple(chunks), bool(carry)),
        out_shape=[sds(1024, 512), sds(2048, 512)],
        in_specs=[VM] * (2 + len(ws)) + ([VM, HBM] if carry else []),
        out_specs=[VM, HBM],
        scratch_shapes=[pltpu.SemaphoreType.DMA((len(ws),))],
        input_output_aliases={n - 1: 1} if carry else {},
        compiler_params=params(12),
        cost_estimate=cost(6 * 1024 * 512 * 256 * len(chunks), 6 << 20),
        name="back",
    )(*ins)


def gram_h_kernel(h_ref, mine_ref, theirs_ref, tmp):
    z, y, _, c = place()
    h = h_ref[...]
    tmp[...] = h.T
    left = tmp[pl.ds(pl.multiple_of(32 * (4 * z + y), 32), 32), :]
    both = dot3(*split(left), *split(h))
    first = (c == 0).astype(f32)
    mine_ref[...] = both[:16] * first + both[16:] * (1.0 - first)
    theirs_ref[...] = both[16:] * first + both[:16] * (1.0 - first)


def gram_h(h):
    return pl.pallas_call(
        gram_h_kernel,
        out_shape=[sds(16, 512)] * 2,
        in_specs=[VM],
        out_specs=[VM] * 2,
        scratch_shapes=[pltpu.VMEM((512, 1024), f32)],
        compiler_params=params(12),
        cost_estimate=cost(6 * 512 * 32 * 1024, 4 << 20),
        name="gram_h",
    )(h)


def gram_w_kernel(w_ref, mine_ref, theirs_ref, tmp):
    z, y, _, c = place()
    w = w_ref[...]
    tmp[...] = dot3(*split(w.T), *split(w))
    for k in range(4):
        for m in range(4):
            s = 4 * ((z + REL[k]) % 4) + (y + REL[m]) % 4
            at = 64 * k + 16 * m
            mine_ref[at : at + 16, :] = tmp[pl.ds(pl.multiple_of(32 * s + 16 * c, 16), 16), :]
            theirs_ref[at : at + 16, :] = tmp[pl.ds(pl.multiple_of(32 * s + 16 * (1 - c), 16), 16), :]


def gram_w(w):
    return pl.pallas_call(
        gram_w_kernel,
        out_shape=[sds(256, 512)] * 2,
        in_specs=[VM],
        out_specs=[VM] * 2,
        scratch_shapes=[pltpu.VMEM((512, 512), f32)],
        compiler_params=params(10),
        cost_estimate=cost(6 * 512 * 512 * 256, 4 << 20),
        name="gram_w",
    )(w)


def sweep_kernel(axis, product, start, mine, theirs, *refs):
    outs, (g, gh, gl, fh, fl, ff, pp, sem) = refs[:-8], refs[-8:]
    z, y, x, c = place()
    n = ff.shape[0]
    first = n * (2 * x + c if axis == "col" else 4 * z + y)
    begin = pltpu.make_async_copy(start.at[pl.ds(pl.multiple_of(first, n), n), :], ff, sem)
    begin.start()
    for t, piece in enumerate((mine, theirs)):
        cc = c if t == 0 else 1 - c
        for j in range(4):
            for i in range(4):
                row = 32 * (4 * ((z + REL[i]) % 4) + (y + REL[j]) % 4) + 16 * cc
                g[pl.ds(pl.multiple_of(row, 16), 16), :] = piece[64 * j + 16 * i : 64 * j + 16 * i + 16, :]
    hi, lo = split(g[...])
    gh[...] = hi
    gl[...] = lo
    inv = []
    for b in range(0, 512, BLOCK):
        inv.append(1.0 / jnp.sum(g[b : b + BLOCK, b : b + BLOCK], axis=0, keepdims=True))
    total = product[:n, :]
    for k in range(n, product.shape[0], n):
        total = total + product[k : k + n, :]
    pp[...] = total
    begin.wait()
    hi, lo = split(ff[...])
    fh[...] = hi
    fl[...] = lo
    for _ in range(SWEEPS):
        for k, b in enumerate(range(0, 512, BLOCK)):
            cols = slice(b, b + BLOCK)
            fg = dot3(fh[...], fl[...], gh[:, cols], gl[:, cols])
            new = jnp.maximum(ff[:, cols] + (pp[:, cols] - fg) * inv[k], floor_value)
            ff[:, cols] = new
            hi, lo = split(new)
            fh[:, cols] = hi
            fl[:, cols] = lo
    n = n // len(outs)
    for k, out in enumerate(outs):
        out[...] = ff[n * k : n * (k + 1), :]


def sweep(product, start, axis, rows, pieces, nout):
    return pl.pallas_call(
        functools.partial(sweep_kernel, axis),
        out_shape=[sds(rows // nout, 512)] * nout,
        in_specs=[VM, HBM, VM, VM],
        out_specs=[VM] * nout,
        scratch_shapes=[
            pltpu.VMEM((512, 512), f32),
            pltpu.VMEM((512, 512), bf16),
            pltpu.VMEM((512, 512), bf16),
            pltpu.VMEM((rows, 512), bf16),
            pltpu.VMEM((rows, 512), bf16),
            pltpu.VMEM((rows, 512), f32),
            pltpu.VMEM((rows, 512), f32),
            pltpu.SemaphoreType.DMA,
        ],
        compiler_params=params(12),
        cost_estimate=cost(72 * rows * 512 * 512, 4 << 20),
        name="sweep",
    )(product, start, *pieces)


def lay_h_kernel(*refs):
    ins, out = refs[:8], refs[8]
    z, y, _, _ = place()
    for half in range(2):
        for j in range(4):
            for i in range(4):
                dz, dy = (REL[i], REL[j]) if half == 0 else (REL[j], REL[i])
                row = pl.multiple_of(64 * (4 * ((z + dz) % 4) + (y + dy) % 4) + 32 * half, 32)
                out[pl.ds(row, 32), :] = ins[4 * half + j][32 * i : 32 * (i + 1), :]


def lay_h(pieces):
    return pl.pallas_call(
        lay_h_kernel,
        out_shape=sds(1024, 512),
        in_specs=[VM] * 8,
        out_specs=VM,
        compiler_params=params(6),
        cost_estimate=cost(0, 4 << 20),
        name="lay_h",
    )(*pieces)


def moves(axis, dim):
    out = {}
    for r in range(4):
        pairs = []
        if axis == "col":
            for i in range(8):
                x, c = i // 2, i % 2
                pairs.append((i, 2 * x + 1 - c) if dim == "core" else (i, 2 * ((x + r) % 4) + c))
        else:
            for i in range(16):
                z, y = i // 4, i % 4
                pairs.append((i, 4 * ((z + r) % 4) + y) if dim == "z" else (i, 4 * z + (y + r) % 4))
        out[r] = pairs
    return out


XGROUPS = [[0, 2, 4, 6], [1, 3, 5, 7]]
CORE, X = moves("col", "core"), moves("col", "x")
Y, Z = moves("samp", "y"), moves("samp", "z")


def swap(a):
    return lax.ppermute(a, "col", CORE[0])


def send(a, axis, table, r):
    return lax.ppermute(a, axis, table[r])


def fetch(a, axis, table):
    return [lax.ppermute(a, axis, table[(4 - r) % 4]) for r in REL[1:]]


def after(a, *others):
    return lax.optimization_barrier((a,) + others)[0]


def join_kernel(nout, *refs):
    ins, outs = refs[:-nout], refs[-nout:]
    n = len(ins) // nout
    for k, out in enumerate(outs):
        rows = ins[n * k].shape[0]
        for i in range(n):
            out[rows * i : rows * (i + 1), :] = ins[n * k + i][...]


def join(parts, nout=1):
    rows = parts[0].shape[0] * len(parts) // nout
    out = pl.pallas_call(
        functools.partial(join_kernel, nout),
        out_shape=[sds(rows, 512)] * nout,
        in_specs=[VM] * len(parts),
        out_specs=[VM] * nout,
        compiler_params=params(4),
        cost_estimate=cost(0, rows * nout * 4096),
        name="join",
    )(*parts)
    return out if nout > 1 else out[0]


def add_kernel(n, *refs):
    total = refs[0][...]
    for r in refs[1:n]:
        total = total + r[...]
    outs = refs[n:]
    rows = total.shape[0] // len(outs)
    for k, out in enumerate(outs):
        out[...] = total[rows * k : rows * (k + 1)]


def add(parts, nout=1):
    rows = parts[0].shape[0]
    out = pl.pallas_call(
        functools.partial(add_kernel, len(parts)),
        out_shape=[sds(rows // nout, 512)] * nout,
        in_specs=[VM] * len(parts),
        out_specs=[VM] * nout,
        compiler_params=params(4),
        cost_estimate=cost(rows * 512 * len(parts), rows * 4096 * len(parts)),
        name="add",
    )(*parts)
    return out if nout > 1 else out[0]


def deal(pieces, axis, table):
    return [pieces[0]] + [send(pieces[k], axis, table, REL[k]) for k in (1, 2, 3)]


def over_all(strip):
    strip = add([strip] + fetch(strip, "col", X))
    strip = join([strip] + fetch(strip, "samp", Z))
    strip = join([strip] + fetch(strip, "samp", Y))
    return strip, swap(strip)


def shards(spectra, w_start, h_start):
    a, hh, hl = prod(spectra, h_start, (0, 1, 2, 3), True)
    recv = swap(a)
    g_mine, g_theirs = gram_h(after(h_start, a))
    g_theirs = swap(g_theirs)
    h = (after(hh, g_mine), hl)
    low = prod(spectra, h, (0, 1), False)
    both = prod(spectra, h, (2, 3), False, (low, recv))
    product = lax.psum_scatter(both, "col", scatter_dimension=0, axis_index_groups=XGROUPS, tiled=True)

    pieces_h = over_all(add([after(g_mine, both), g_theirs]))

    (w,) = sweep(product, w_start, "col", 256, pieces_h, 1)

    ws = swap(w)
    near_p, near_m, far = fetch(w, "col", X)

    g_mine, g_theirs = gram_w(w)
    flipped = flip(after(spectra, g_theirs))
    strips = add([g_mine, after(swap(g_theirs), *flipped)], 4)
    strips = deal(strips, "samp", Z)
    carry = back(flipped, (w, ws), ((0, False), (0, True)))
    strips = add([after(strips[0], carry[0])] + strips[1:], 4)
    strips = deal(strips, "samp", Y)
    sib_p, sib_m = swap(after(near_p, *strips)), swap(near_m)
    carry = back(flipped, (near_p, near_m), ((1, False), (3, False)), carry)
    strip = add([after(strips[0], carry[0])] + strips[1:])
    carry = back(flipped, (sib_p, sib_m), ((1, True), (3, True)), carry)
    sib_f = swap(far)
    back_sum, w_out = back(flipped, (far, sib_f), ((2, False), (2, True)), carry)

    product = lax.all_to_all(back_sum, "samp", 0, 0, tiled=True)
    pieces_w = over_all(after(strip, back_sum))
    ha, hb = sweep(product, h_start, "samp", 64, pieces_w, 2)

    row_a, row_b = join([ha] + fetch(ha, "samp", Z) + [hb] + fetch(hb, "samp", Y), 2)
    h_out = lay_h([row_a] + fetch(row_a, "samp", Y) + [row_b] + fetch(row_b, "samp", Z))
    return (w_out, h_out)


def solution(mesh):
    return jax.shard_map(
        shards,
        mesh=mesh,
        in_specs=(P("samp", "col"), P("samp", None), P("col", None)),
        out_specs=(P("samp", None), P("col", None)),
        check_vma=False,
    )
```

```python
import functools
import jax
import jax.numpy as jnp
from jax import lax
from jax.experimental import pallas as pl
from jax.experimental.pallas import tpu as pltpu
from jax.sharding import PartitionSpec as P

BLOCK = 128
SWEEPS = 3
floor_value = 1e-06
REL = (0, 1, 3, 2)
f32, bf16 = jnp.float32, jnp.bfloat16
ANY = pl.BlockSpec(memory_space=pl.ANY)
HBM = pl.BlockSpec(memory_space=pltpu.HBM)
VM = pl.BlockSpec(memory_space=pltpu.VMEM)


def sds(*shape, dtype=f32):
    return jax.ShapeDtypeStruct(shape, dtype)


def cost(flops, nbytes):
    return pl.CostEstimate(flops=flops, bytes_accessed=nbytes, transcendentals=0)


def params(mib):
    return pltpu.CompilerParams(vmem_limit_bytes=mib << 20)


def split(a):
    hi = a.astype(bf16)
    return hi, (a - hi.astype(f32)).astype(bf16)


def dot3(ah, al, bh, bl):
    d = functools.partial(jnp.dot, preferred_element_type=f32)
    return d(ah, bh) + (d(ah, bl) + d(al, bh))


def place():
    s, q = lax.axis_index("samp"), lax.axis_index("col")
    return s // 4, s % 4, q // 2, q % 2


def prod_kernel(chunks, sibling, first, recv, last, *refs):
    refs = list(refs)
    x_ref = refs.pop(0)
    if first:
        h_ref = refs.pop(0)
    else:
        hh_ref, hl_ref = refs.pop(0), refs.pop(0)
    recv_ref = refs.pop(0) if recv else None
    low_ref = refs.pop(0) if last else None
    out_ref = refs.pop(0)
    if first:
        hh_ref, hl_ref = refs.pop(0), refs.pop(0)
        hh, hl = split(h_ref[...])
        hh_ref[...] = hh
        hl_ref[...] = hl
    _, _, _, c = place()
    cc = 1 - c if sibling else c
    if last:
        tmp, sem = refs
        low = pltpu.make_async_copy(low_ref, out_ref.at[pl.ds(0, 512), :], sem.at[0])
        low.start()
    rows = [x_ref[pl.ds(pl.multiple_of(512 * k + 256 * cc, 256), 256), :] for k in chunks]
    ah, al = split(jnp.concatenate(rows, axis=0))
    out = dot3(ah, al, hh_ref[...], hl_ref[...])
    if recv:
        out = out + recv_ref[...]
    if last:
        tmp[...] = out
        high = pltpu.make_async_copy(tmp, out_ref.at[pl.ds(512, 512), :], sem.at[1])
        high.start()
        low.wait()
        high.wait()
    else:
        out_ref[...] = out


def prod(spectra, h, chunks, sibling, recv=None, low=None):
    first = not isinstance(h, tuple)
    last = low is not None
    ins = [spectra] + ([h] if first else list(h)) + ([] if recv is None else [recv]) + ([low] if last else [])
    outs = [sds(1024 if last else 512, 512)]
    if first:
        outs += [sds(1024, 512, dtype=bf16)] * 2
    out = pl.pallas_call(
        functools.partial(prod_kernel, chunks, sibling, first, recv is not None, last),
        out_shape=outs,
        in_specs=[VM] * len(ins),
        out_specs=[HBM] if last else [VM] * len(outs),
        scratch_shapes=[pltpu.VMEM((512, 512), f32), pltpu.SemaphoreType.DMA((2,))] if last else [],
        compiler_params=params(14),
        cost_estimate=cost(6 * 512 * 1024 * 512, 6 << 20),
        name="prod",
    )(*ins)
    return out if first else out[0]


def flip_kernel(x_ref, th_ref, tl_ref):
    for k in range(0, 1024, 128):
        hi, lo = split(x_ref[:, k : k + 128].T)
        th_ref[0, k : k + 128, :] = hi
        tl_ref[0, k : k + 128, :] = lo


def flip(spectra):
    spec = pl.BlockSpec((1, 1024, 128), lambda i: (i, 0, 0))
    return pl.pallas_call(
        flip_kernel,
        grid=(16,),
        out_shape=[sds(16, 1024, 128, dtype=bf16)] * 2,
        in_specs=[pl.BlockSpec((128, 1024), lambda i: (i, 0))],
        out_specs=[spec, spec],
        compiler_params=params(44),
        cost_estimate=cost(1 << 24, 16 << 20),
        name="flip",
    )(spectra)


def back_kernel(chunks, later, *refs):
    refs = list(refs)
    th_ref, tl_ref = refs.pop(0), refs.pop(0)
    ws = [refs.pop(0) for _ in chunks]
    acc_ref = refs.pop(0) if later else None
    if later:
        refs.pop(0)
    out_ref, w_out, sem = refs[:3]
    z, y, x, c = place()
    at, copies = [], []
    for k, (r, sibling) in enumerate(chunks):
        first = 2 * (2 * ((x + r) % 4) + (1 - c if sibling else c))
        at += [first, first + 1]
        cp = pltpu.make_async_copy(ws[k], w_out.at[pl.ds(pl.multiple_of(128 * first, 256), 256), :], sem.at[k])
        cp.start()
        copies.append(cp)
    wh, wl = split(jnp.concatenate([w[...] for w in ws], axis=0))
    for k in range(0, 1024, 512):
        rows = slice(k, k + 512)
        ah = jnp.concatenate([th_ref[i, rows, :] for i in at], axis=1)
        al = jnp.concatenate([tl_ref[i, rows, :] for i in at], axis=1)
        out = dot3(ah, al, wh, wl)
        if later:
            out = out + acc_ref[rows, :]
        if len(refs) > 3:
            refs[3][rows, :] = out
            cp = pltpu.make_async_copy(refs[3].at[rows, :], out_ref.at[rows, :], sem.at[2 + k // 512])
            cp.start()
            copies.append(cp)
        else:
            out_ref[rows, :] = out
    for cp in copies:
        cp.wait()


def back(flipped, ws, chunks, carry=(), last=False):
    ins = list(flipped) + list(ws) + list(carry)
    n = len(ins)
    return pl.pallas_call(
        functools.partial(back_kernel, tuple(chunks), bool(carry)),
        out_shape=[sds(1024, 512), sds(2048, 512)],
        in_specs=[VM] * (2 + len(ws)) + ([VM, HBM] if carry else []),
        out_specs=[HBM if last else VM, HBM],
        scratch_shapes=[pltpu.SemaphoreType.DMA((4,))] + ([pltpu.VMEM((1024, 512), f32)] if last else []),
        input_output_aliases={n - 1: 1} if carry else {},
        compiler_params=params(12),
        cost_estimate=cost(6 * 1024 * 512 * 256 * len(chunks), 6 << 20),
        name="back",
    )(*ins)


def gram_h_kernel(h_ref, mine_ref, theirs_ref, tmp):
    z, y, _, c = place()
    h = h_ref[...]
    tmp[...] = h.T
    left = tmp[pl.ds(pl.multiple_of(32 * (4 * z + y), 32), 32), :]
    both = dot3(*split(left), *split(h))
    first = (c == 0).astype(f32)
    mine_ref[...] = both[:16] * first + both[16:] * (1.0 - first)
    theirs_ref[...] = both[16:] * first + both[:16] * (1.0 - first)


def gram_h(h):
    return pl.pallas_call(
        gram_h_kernel,
        out_shape=[sds(16, 512)] * 2,
        in_specs=[VM],
        out_specs=[VM] * 2,
        scratch_shapes=[pltpu.VMEM((512, 1024), f32)],
        compiler_params=params(12),
        cost_estimate=cost(6 * 512 * 32 * 1024, 4 << 20),
        name="gram_h",
    )(h)


def gram_w_kernel(w_ref, mine_ref, theirs_ref, tmp):
    _, _, x, c = place()
    w = w_ref[...]
    tmp[...] = dot3(*split(w.T), *split(w))
    for k in range(4):
        row = 128 * ((x + REL[k]) % 4)
        rows = slice(64 * k, 64 * (k + 1))
        mine_ref[rows, :] = tmp[pl.ds(pl.multiple_of(row + 64 * c, 64), 64), :]
        theirs_ref[rows, :] = tmp[pl.ds(pl.multiple_of(row + 64 * (1 - c), 64), 64), :]


def gram_w(w):
    return pl.pallas_call(
        gram_w_kernel,
        out_shape=[sds(256, 512)] * 2,
        in_specs=[VM],
        out_specs=[VM] * 2,
        scratch_shapes=[pltpu.VMEM((512, 512), f32)],
        compiler_params=params(10),
        cost_estimate=cost(6 * 512 * 512 * 256, 4 << 20),
        name="gram_w",
    )(w)


def sweep_kernel(axis, product, start, mine, theirs, *refs):
    outs, (g, gh, gl, fh, fl, ff, pp, sem) = refs[:-8], refs[-8:]
    z, y, x, c = place()
    n = ff.shape[0]
    first = n * (2 * x + c if axis == "col" else 4 * z + y)
    begin = pltpu.make_async_copy(start.at[pl.ds(pl.multiple_of(first, n), n), :], ff, sem)
    begin.start()
    for t, piece in enumerate((mine, theirs)):
        cc = c if t == 0 else 1 - c
        for j in range(4):
            if axis == "samp":
                row = 128 * ((x + REL[j]) % 4) + 64 * cc
                g[pl.ds(pl.multiple_of(row, 64), 64), :] = piece[64 * j : 64 * j + 64, :]
                continue
            for i in range(4):
                row = 32 * (4 * ((z + REL[i]) % 4) + (y + REL[j]) % 4) + 16 * cc
                g[pl.ds(pl.multiple_of(row, 16), 16), :] = piece[64 * j + 16 * i : 64 * j + 16 * i + 16, :]
    hi, lo = split(g[...])
    gh[...] = hi
    gl[...] = lo
    inv = []
    for b in range(0, 512, BLOCK):
        inv.append(1.0 / jnp.sum(g[b : b + BLOCK, b : b + BLOCK], axis=0, keepdims=True))
    total = product[:n, :]
    for k in range(n, product.shape[0], n):
        total = total + product[k : k + n, :]
    pp[...] = total
    begin.wait()
    hi, lo = split(ff[...])
    fh[...] = hi
    fl[...] = lo
    for _ in range(SWEEPS):
        for k, b in enumerate(range(0, 512, BLOCK)):
            cols = slice(b, b + BLOCK)
            fg = dot3(fh[...], fl[...], gh[:, cols], gl[:, cols])
            new = jnp.maximum(ff[:, cols] + (pp[:, cols] - fg) * inv[k], floor_value)
            ff[:, cols] = new
            hi, lo = split(new)
            fh[:, cols] = hi
            fl[:, cols] = lo
    n = n // len(outs)
    for k, out in enumerate(outs):
        out[...] = ff[n * k : n * (k + 1), :]


def sweep(product, start, axis, rows, pieces, nout):
    return pl.pallas_call(
        functools.partial(sweep_kernel, axis),
        out_shape=[sds(rows // nout, 512)] * nout,
        in_specs=[VM, HBM, VM, VM],
        out_specs=[VM] * nout,
        scratch_shapes=[
            pltpu.VMEM((512, 512), f32),
            pltpu.VMEM((512, 512), bf16),
            pltpu.VMEM((512, 512), bf16),
            pltpu.VMEM((rows, 512), bf16),
            pltpu.VMEM((rows, 512), bf16),
            pltpu.VMEM((rows, 512), f32),
            pltpu.VMEM((rows, 512), f32),
            pltpu.SemaphoreType.DMA,
        ],
        compiler_params=params(50),
        cost_estimate=cost(72 * rows * 512 * 512, 4 << 20),
        name="sweep",
    )(product, start, *pieces)


def lay_h_kernel(*refs):
    ins, out = refs[:8], refs[8]
    z, y, _, _ = place()
    for half in range(2):
        for j in range(4):
            for i in range(4):
                dz, dy = (REL[i], REL[j]) if half == 0 else (REL[j], REL[i])
                row = pl.multiple_of(64 * (4 * ((z + dz) % 4) + (y + dy) % 4) + 32 * half, 32)
                out[pl.ds(row, 32), :] = ins[4 * half + j][32 * i : 32 * (i + 1), :]


def lay_h(pieces):
    return pl.pallas_call(
        lay_h_kernel,
        out_shape=sds(1024, 512),
        in_specs=[VM] * 8,
        out_specs=VM,
        compiler_params=params(6),
        cost_estimate=cost(0, 4 << 20),
        name="lay_h",
    )(*pieces)


def moves(axis, dim):
    out = {}
    for r in range(4):
        pairs = []
        if axis == "col":
            for i in range(8):
                x, c = i // 2, i % 2
                pairs.append((i, 2 * x + 1 - c) if dim == "core" else (i, 2 * ((x + r) % 4) + c))
        else:
            for i in range(16):
                z, y = i // 4, i % 4
                pairs.append((i, 4 * ((z + r) % 4) + y) if dim == "z" else (i, 4 * z + (y + r) % 4))
        out[r] = pairs
    return out


XGROUPS = [[0, 2, 4, 6], [1, 3, 5, 7]]
CORE, X = moves("col", "core"), moves("col", "x")
Y, Z = moves("samp", "y"), moves("samp", "z")
Y_PAIRS = [[(i, i ^ k) for i in range(16)] for k in (1, 3)]
Z_PAIRS = [[(i, i ^ k) for i in range(16)] for k in (4, 12)]


def swap(a):
    return lax.ppermute(a, "col", CORE[0])


def send(a, axis, table, r):
    return lax.ppermute(a, axis, table[r])


def fetch(a, axis, table):
    return [lax.ppermute(a, axis, table[(4 - r) % 4]) for r in REL[1:]]


def after(a, *others):
    return lax.optimization_barrier((a,) + others)[0]


def join_kernel(nout, *refs):
    ins, outs = refs[:-nout], refs[-nout:]
    n = len(ins) // nout
    for k, out in enumerate(outs):
        rows = ins[n * k].shape[0]
        for i in range(n):
            out[rows * i : rows * (i + 1), :] = ins[n * k + i][...]


def join(parts, nout=1):
    rows = parts[0].shape[0] * len(parts) // nout
    out = pl.pallas_call(
        functools.partial(join_kernel, nout),
        out_shape=[sds(rows, 512)] * nout,
        in_specs=[VM] * len(parts),
        out_specs=[VM] * nout,
        compiler_params=params(4),
        cost_estimate=cost(0, rows * nout * 4096),
        name="join",
    )(*parts)
    return out if nout > 1 else out[0]


def add_kernel(n, *refs):
    total = refs[0][...]
    for r in refs[1:n]:
        total = total + r[...]
    outs = refs[n:]
    rows = total.shape[0] // len(outs)
    for k, out in enumerate(outs):
        out[...] = total[rows * k : rows * (k + 1)]


def add(parts, nout=1):
    rows = parts[0].shape[0]
    out = pl.pallas_call(
        functools.partial(add_kernel, len(parts)),
        out_shape=[sds(rows // nout, 512)] * nout,
        in_specs=[VM] * len(parts),
        out_specs=[VM] * nout,
        compiler_params=params(4),
        cost_estimate=cost(rows * 512 * len(parts), rows * 4096 * len(parts)),
        name="add",
    )(*parts)
    return out if nout > 1 else out[0]


def deal(pieces, axis, table):
    return [pieces[0]] + [send(pieces[k], axis, table, REL[k]) for k in (1, 2, 3)]


def pair_sum(a, pairs):
    return add([a, lax.ppermute(a, "samp", pairs)])


def over_all(strip):
    strip = add([strip] + fetch(strip, "col", X))
    strip = join([strip] + fetch(strip, "samp", Z))
    strip = join([strip] + fetch(strip, "samp", Y))
    return strip, swap(strip)


def shards(spectra, w_start, h_start):
    g_mine, g_theirs = gram_h(h_start)
    a1, hh, hl = prod(spectra, after(h_start, g_mine), (0, 1), True)
    r1 = swap(a1)
    h = (hh, hl)
    a2 = prod(spectra, h, (2, 3), True)
    r2 = swap(a2)
    g_theirs = swap(g_theirs)
    low = prod(spectra, h, (0, 1), False, after(r1, a2))
    both = prod(spectra, h, (2, 3), False, r2, low)
    product = lax.all_to_all(both, "col", 0, 0, axis_index_groups=XGROUPS, tiled=True)

    pieces_h = over_all(add([after(g_mine, both), g_theirs]))

    (w,) = sweep(product, w_start, "col", 256, pieces_h, 1)

    ws = swap(w)
    near_p, near_m, far = fetch(w, "col", X)

    g_mine, g_theirs = gram_w(w)
    flipped = flip(after(spectra, g_theirs))
    slices = deal(add([g_mine, after(swap(g_theirs), *flipped)], 4), "col", X)
    carry = back(flipped, (w, ws), ((0, False), (0, True)))
    part = add([after(slices[0], carry[0])] + slices[1:])
    part = pair_sum(part, Y_PAIRS[0])
    sib_p, sib_m = swap(after(near_p, part)), swap(after(near_m, part))
    part = pair_sum(part, Y_PAIRS[1])
    carry = back(flipped, (near_p, near_m), ((1, False), (3, False)), (after(carry[0], part), carry[1]))
    part = pair_sum(after(part, carry[0]), Z_PAIRS[0])
    carry = back(flipped, (sib_p, sib_m), ((1, True), (3, True)), (after(carry[0], part), carry[1]))
    part = pair_sum(after(part, carry[0]), Z_PAIRS[1])
    sib_f = swap(far)
    back_sum, w_out = back(flipped, (far, sib_f), ((2, False), (2, True)), carry, True)

    product = lax.all_to_all(back_sum, "samp", 0, 0, tiled=True)
    part = join([after(part, back_sum)] + fetch(part, "col", X))
    ha, hb = sweep(product, h_start, "samp", 64, (part, swap(part)), 2)

    row_a, row_b = join([ha] + fetch(ha, "samp", Z) + [hb] + fetch(hb, "samp", Y), 2)
    h_out = lay_h([row_a] + fetch(row_a, "samp", Y) + [row_b] + fetch(row_b, "samp", Z))
    return (w_out, h_out)


def solution(mesh):
    return jax.shard_map(
        shards,
        mesh=mesh,
        in_specs=(P("samp", "col"), P("samp", None), P("col", None)),
        out_specs=(P("samp", None), P("col", None)),
        check_vma=False,
    )
```

```python
import functools
import jax
import jax.numpy as jnp
from jax import lax
from jax.experimental import pallas as pl
from jax.experimental.pallas import tpu as pltpu
from jax.sharding import PartitionSpec as P

BLOCK = 128
SWEEPS = 3
floor_value = 1e-06
REL = (0, 1, 3, 2)
f32, bf16 = jnp.float32, jnp.bfloat16
ANY = pl.BlockSpec(memory_space=pl.ANY)
HBM = pl.BlockSpec(memory_space=pltpu.HBM)
VM = pl.BlockSpec(memory_space=pltpu.VMEM)


def sds(*shape, dtype=f32):
    return jax.ShapeDtypeStruct(shape, dtype)


def cost(flops, nbytes):
    return pl.CostEstimate(flops=flops, bytes_accessed=nbytes, transcendentals=0)


def params(mib):
    return pltpu.CompilerParams(vmem_limit_bytes=mib << 20)


def split(a):
    hi = a.astype(bf16)
    return hi, (a - hi.astype(f32)).astype(bf16)


def dot3(ah, al, bh, bl):
    d = functools.partial(jnp.dot, preferred_element_type=f32)
    return d(ah, bh) + (d(ah, bl) + d(al, bh))


def place():
    s, q = lax.axis_index("samp"), lax.axis_index("col")
    return s // 4, s % 4, q // 2, q % 2


def prod_kernel(chunks, sibling, first, recv, last, *refs):
    refs = list(refs)
    x_ref = refs.pop(0)
    if first:
        h_ref = refs.pop(0)
    else:
        hh_ref, hl_ref = refs.pop(0), refs.pop(0)
    recv_ref = refs.pop(0) if recv else None
    low_ref = refs.pop(0) if last else None
    out_ref = refs.pop(0)
    if first:
        hh_ref, hl_ref = refs.pop(0), refs.pop(0)
        hh, hl = split(h_ref[...])
        hh_ref[...] = hh
        hl_ref[...] = hl
    _, _, _, c = place()
    cc = 1 - c if sibling else c
    if last:
        tmp, sem = refs
        low = pltpu.make_async_copy(low_ref, out_ref.at[pl.ds(0, 512), :], sem.at[0])
        low.start()
    rows = [x_ref[pl.ds(pl.multiple_of(512 * k + 256 * cc, 256), 256), :] for k in chunks]
    ah, al = split(jnp.concatenate(rows, axis=0))
    out = dot3(ah, al, hh_ref[...], hl_ref[...])
    if recv:
        out = out + recv_ref[...]
    if last:
        tmp[...] = out
        high = pltpu.make_async_copy(tmp, out_ref.at[pl.ds(512, 512), :], sem.at[1])
        high.start()
        low.wait()
        high.wait()
    else:
        out_ref[...] = out


def prod(spectra, h, chunks, sibling, recv=None, low=None):
    first = not isinstance(h, tuple)
    last = low is not None
    ins = [spectra] + ([h] if first else list(h)) + ([] if recv is None else [recv]) + ([low] if last else [])
    outs = [sds(1024 if last else 512, 512)]
    if first:
        outs += [sds(1024, 512, dtype=bf16)] * 2
    out = pl.pallas_call(
        functools.partial(prod_kernel, chunks, sibling, first, recv is not None, last),
        out_shape=outs,
        in_specs=[VM] * len(ins),
        out_specs=[HBM] if last else [VM] * len(outs),
        scratch_shapes=[pltpu.VMEM((512, 512), f32), pltpu.SemaphoreType.DMA((2,))] if last else [],
        compiler_params=params(14),
        cost_estimate=cost(6 * 512 * 1024 * 512, 6 << 20),
        name="prod",
    )(*ins)
    return out if first else out[0]


def flip_kernel(x_ref, th_ref, tl_ref):
    for k in range(0, 1024, 128):
        hi, lo = split(x_ref[:, k : k + 128].T)
        th_ref[0, k : k + 128, :] = hi
        tl_ref[0, k : k + 128, :] = lo


def flip(spectra):
    spec = pl.BlockSpec((1, 1024, 128), lambda i: (i, 0, 0))
    return pl.pallas_call(
        flip_kernel,
        grid=(16,),
        out_shape=[sds(16, 1024, 128, dtype=bf16)] * 2,
        in_specs=[pl.BlockSpec((128, 1024), lambda i: (i, 0))],
        out_specs=[spec, spec],
        compiler_params=params(6),
        cost_estimate=cost(1 << 24, 16 << 20),
        name="flip",
    )(spectra)


def back_kernel(chunks, later, *refs):
    refs = list(refs)
    th_ref, tl_ref = refs.pop(0), refs.pop(0)
    ws = [refs.pop(0) for _ in chunks]
    acc_ref = refs.pop(0) if later else None
    if later:
        refs.pop(0)
    out_ref, w_out, sem = refs[:3]
    z, y, x, c = place()
    at, copies = [], []
    for k, (r, sibling) in enumerate(chunks):
        first = 2 * (2 * ((x + r) % 4) + (1 - c if sibling else c))
        at += [first, first + 1]
        cp = pltpu.make_async_copy(ws[k], w_out.at[pl.ds(pl.multiple_of(128 * first, 256), 256), :], sem.at[k])
        cp.start()
        copies.append(cp)
    wh, wl = split(jnp.concatenate([w[...] for w in ws], axis=0))
    for k in range(0, 1024, 512):
        rows = slice(k, k + 512)
        ah = jnp.concatenate([th_ref[i, rows, :] for i in at], axis=1)
        al = jnp.concatenate([tl_ref[i, rows, :] for i in at], axis=1)
        out = dot3(ah, al, wh, wl)
        if later:
            out = out + acc_ref[rows, :]
        if len(refs) > 3:
            refs[3][rows, :] = out
            cp = pltpu.make_async_copy(refs[3].at[rows, :], out_ref.at[rows, :], sem.at[2 + k // 512])
            cp.start()
            copies.append(cp)
        else:
            out_ref[rows, :] = out
    for cp in copies:
        cp.wait()


def back(flipped, ws, chunks, carry=(), last=False):
    ins = list(flipped) + list(ws) + list(carry)
    n = len(ins)
    return pl.pallas_call(
        functools.partial(back_kernel, tuple(chunks), bool(carry)),
        out_shape=[sds(1024, 512), sds(2048, 512)],
        in_specs=[VM] * (2 + len(ws)) + ([VM, HBM] if carry else []),
        out_specs=[HBM if last else VM, HBM],
        scratch_shapes=[pltpu.SemaphoreType.DMA((4,))] + ([pltpu.VMEM((1024, 512), f32)] if last else []),
        input_output_aliases={n - 1: 1} if carry else {},
        compiler_params=params(12),
        cost_estimate=cost(6 * 1024 * 512 * 256 * len(chunks), 6 << 20),
        name="back",
    )(*ins)


def gram_h_kernel(h_ref, mine_ref, theirs_ref, tmp):
    z, y, _, c = place()
    h = h_ref[...]
    tmp[...] = h.T
    left = tmp[pl.ds(pl.multiple_of(32 * (4 * z + y), 32), 32), :]
    both = dot3(*split(left), *split(h))
    first = (c == 0).astype(f32)
    mine_ref[...] = both[:16] * first + both[16:] * (1.0 - first)
    theirs_ref[...] = both[16:] * first + both[:16] * (1.0 - first)


def gram_h(h):
    return pl.pallas_call(
        gram_h_kernel,
        out_shape=[sds(16, 512)] * 2,
        in_specs=[VM],
        out_specs=[VM] * 2,
        scratch_shapes=[pltpu.VMEM((512, 1024), f32)],
        compiler_params=params(12),
        cost_estimate=cost(6 * 512 * 32 * 1024, 4 << 20),
        name="gram_h",
    )(h)


def gram_w_kernel(w_ref, mine_ref, theirs_ref, tmp):
    z, y, _, c = place()
    w = w_ref[...]
    tmp[...] = dot3(*split(w.T), *split(w))
    for k in range(4):
        for m in range(4):
            s = 4 * ((z + REL[k]) % 4) + (y + REL[m]) % 4
            at = 64 * k + 16 * m
            mine_ref[at : at + 16, :] = tmp[pl.ds(pl.multiple_of(32 * s + 16 * c, 16), 16), :]
            theirs_ref[at : at + 16, :] = tmp[pl.ds(pl.multiple_of(32 * s + 16 * (1 - c), 16), 16), :]


def gram_w(w):
    return pl.pallas_call(
        gram_w_kernel,
        out_shape=[sds(256, 512)] * 2,
        in_specs=[VM],
        out_specs=[VM] * 2,
        scratch_shapes=[pltpu.VMEM((512, 512), f32)],
        compiler_params=params(10),
        cost_estimate=cost(6 * 512 * 512 * 256, 4 << 20),
        name="gram_w",
    )(w)


def sweep_kernel(axis, product, start, mine, theirs, *refs):
    outs, (g, gh, gl, fh, fl, ff, pp, sem) = refs[:-8], refs[-8:]
    z, y, x, c = place()
    n = ff.shape[0]
    if axis == "col":
        rows = start
    else:
        rows = start.at[pl.ds(pl.multiple_of(n * (4 * z + y), n), n), :]
    begin = pltpu.make_async_copy(rows, ff, sem)
    begin.start()
    for t, piece in enumerate((mine, theirs)):
        cc = c if t == 0 else 1 - c
        for j in range(4):
            for i in range(4):
                row = 32 * (4 * ((z + REL[i]) % 4) + (y + REL[j]) % 4) + 16 * cc
                g[pl.ds(pl.multiple_of(row, 16), 16), :] = piece[64 * j + 16 * i : 64 * j + 16 * i + 16, :]
    hi, lo = split(g[...])
    gh[...] = hi
    gl[...] = lo
    inv = []
    for b in range(0, 512, BLOCK):
        inv.append(1.0 / jnp.sum(g[b : b + BLOCK, b : b + BLOCK], axis=0, keepdims=True))
    total = product[:n, :]
    for k in range(n, product.shape[0], n):
        total = total + product[k : k + n, :]
    pp[...] = total
    begin.wait()
    hi, lo = split(ff[...])
    fh[...] = hi
    fl[...] = lo
    for _ in range(SWEEPS):
        for k, b in enumerate(range(0, 512, BLOCK)):
            cols = slice(b, b + BLOCK)
            fg = dot3(fh[...], fl[...], gh[:, cols], gl[:, cols])
            new = jnp.maximum(ff[:, cols] + (pp[:, cols] - fg) * inv[k], floor_value)
            ff[:, cols] = new
            hi, lo = split(new)
            fh[:, cols] = hi
            fl[:, cols] = lo
    n = n // len(outs)
    for k, out in enumerate(outs):
        out[...] = ff[n * k : n * (k + 1), :]


def sweep(product, start, axis, rows, pieces, nout):
    return pl.pallas_call(
        functools.partial(sweep_kernel, axis),
        out_shape=[sds(rows // nout, 512)] * nout,
        in_specs=[VM, VM if axis == "col" else HBM, VM, VM],
        out_specs=[VM] * nout,
        scratch_shapes=[
            pltpu.VMEM((512, 512), f32),
            pltpu.VMEM((512, 512), bf16),
            pltpu.VMEM((512, 512), bf16),
            pltpu.VMEM((rows, 512), bf16),
            pltpu.VMEM((rows, 512), bf16),
            pltpu.VMEM((rows, 512), f32),
            pltpu.VMEM((rows, 512), f32),
            pltpu.SemaphoreType.DMA,
        ],
        compiler_params=params(12 if axis == "col" else 50),
        cost_estimate=cost(72 * rows * 512 * 512, 4 << 20),
        name="sweep",
    )(product, start, *pieces)


def take_kernel(w_ref, out_ref, sem):
    _, _, x, c = place()
    rows = w_ref.at[pl.ds(pl.multiple_of(256 * (2 * x + c), 256), 256), :]
    cp = pltpu.make_async_copy(rows, out_ref, sem)
    cp.start()
    cp.wait()


def take(w_start):
    return pl.pallas_call(
        take_kernel,
        out_shape=sds(256, 512),
        in_specs=[HBM],
        out_specs=VM,
        scratch_shapes=[pltpu.SemaphoreType.DMA],
        compiler_params=params(57),
        cost_estimate=cost(0, 1 << 20),
        name="take",
    )(w_start)


def lay_h_kernel(*refs):
    ins, out = refs[:8], refs[8]
    z, y, _, _ = place()
    for half in range(2):
        for j in range(4):
            for i in range(4):
                dz, dy = (REL[i], REL[j]) if half == 0 else (REL[j], REL[i])
                row = pl.multiple_of(64 * (4 * ((z + dz) % 4) + (y + dy) % 4) + 32 * half, 32)
                out[pl.ds(row, 32), :] = ins[4 * half + j][32 * i : 32 * (i + 1), :]


def lay_h(pieces):
    return pl.pallas_call(
        lay_h_kernel,
        out_shape=sds(1024, 512),
        in_specs=[VM] * 8,
        out_specs=VM,
        compiler_params=params(6),
        cost_estimate=cost(0, 4 << 20),
        name="lay_h",
    )(*pieces)


def moves(axis, dim):
    out = {}
    for r in range(4):
        pairs = []
        if axis == "col":
            for i in range(8):
                x, c = i // 2, i % 2
                pairs.append((i, 2 * x + 1 - c) if dim == "core" else (i, 2 * ((x + r) % 4) + c))
        else:
            for i in range(16):
                z, y = i // 4, i % 4
                pairs.append((i, 4 * ((z + r) % 4) + y) if dim == "z" else (i, 4 * z + (y + r) % 4))
        out[r] = pairs
    return out


XGROUPS = [[0, 2, 4, 6], [1, 3, 5, 7]]
CORE, X = moves("col", "core"), moves("col", "x")
Y, Z = moves("samp", "y"), moves("samp", "z")


def swap(a):
    return lax.ppermute(a, "col", CORE[0])


def send(a, axis, table, r):
    return lax.ppermute(a, axis, table[r])


def fetch(a, axis, table):
    return [lax.ppermute(a, axis, table[(4 - r) % 4]) for r in REL[1:]]


def after(a, *others):
    return lax.optimization_barrier((a,) + others)[0]


def join_kernel(nout, *refs):
    ins, outs = refs[:-nout], refs[-nout:]
    n = len(ins) // nout
    for k, out in enumerate(outs):
        rows = ins[n * k].shape[0]
        for i in range(n):
            out[rows * i : rows * (i + 1), :] = ins[n * k + i][...]


def join(parts, nout=1):
    rows = parts[0].shape[0] * len(parts) // nout
    out = pl.pallas_call(
        functools.partial(join_kernel, nout),
        out_shape=[sds(rows, 512)] * nout,
        in_specs=[VM] * len(parts),
        out_specs=[VM] * nout,
        compiler_params=params(4),
        cost_estimate=cost(0, rows * nout * 4096),
        name="join",
    )(*parts)
    return out if nout > 1 else out[0]


def add_kernel(n, *refs):
    total = refs[0][...]
    for r in refs[1:n]:
        total = total + r[...]
    outs = refs[n:]
    rows = total.shape[0] // len(outs)
    for k, out in enumerate(outs):
        out[...] = total[rows * k : rows * (k + 1)]


def add(parts, nout=1):
    rows = parts[0].shape[0]
    out = pl.pallas_call(
        functools.partial(add_kernel, len(parts)),
        out_shape=[sds(rows // nout, 512)] * nout,
        in_specs=[VM] * len(parts),
        out_specs=[VM] * nout,
        compiler_params=params(4),
        cost_estimate=cost(rows * 512 * len(parts), rows * 4096 * len(parts)),
        name="add",
    )(*parts)
    return out if nout > 1 else out[0]


def deal(pieces, axis, table):
    return [pieces[0]] + [send(pieces[k], axis, table, REL[k]) for k in (1, 2, 3)]


def spread(strip):
    strip = join([strip] + fetch(strip, "samp", Z))
    return join([strip] + fetch(strip, "samp", Y))


def shards(spectra, w_start, h_start):
    g_mine, g_theirs = gram_h(h_start)
    strip = add([g_mine, swap(g_theirs)])

    a1, hh, hl = prod(spectra, after(h_start, strip), (0, 1), True)
    r1 = swap(a1)
    h = (hh, hl)
    a2 = prod(spectra, h, (2, 3), True)
    r2 = swap(a2)
    low = prod(spectra, h, (0, 1), False, after(r1, a2))
    strip = add([strip] + fetch(strip, "col", X))
    both = prod(spectra, h, (2, 3), False, r2, after(low, strip))
    product = lax.all_to_all(both, "col", 0, 0, axis_index_groups=XGROUPS, tiled=True)

    part = spread(after(strip, both))
    w0 = take(after(w_start, part))
    (w,) = sweep(product, w0, "col", 256, (part, swap(part)), 1)

    ws = swap(w)
    near_p, near_m, far = fetch(w, "col", X)

    g_mine, g_theirs = gram_w(w)
    flipped = flip(after(spectra, g_theirs))
    strips = add([g_mine, after(swap(g_theirs), *flipped)], 4)
    strips = deal(strips, "samp", Z)
    carry = back(flipped, (w, ws), ((0, False), (0, True)))
    strips = add([after(strips[0], carry[0])] + strips[1:], 4)
    strips = deal(strips, "samp", Y)
    sib_p, sib_m = swap(after(near_p, *strips)), swap(after(near_m, *strips))
    strip = add(strips)
    carry = back(flipped, (near_p, near_m), ((1, False), (3, False)), (after(carry[0], strip), carry[1]))
    part = join([after(strip, carry[0])] + fetch(strip, "samp", Z))
    carry = back(flipped, (sib_p, sib_m), ((1, True), (3, True)), (after(carry[0], part), carry[1]))
    sib_f = swap(after(far, part))
    part = join([after(part, carry[0])] + fetch(part, "samp", Y))
    carry = (after(carry[0], part), carry[1])
    back_sum, w_out = back(flipped, (far, sib_f), ((2, False), (2, True)), carry, True)

    product = lax.all_to_all(back_sum, "samp", 0, 0, tiled=True)
    part = after(part, back_sum)
    part = add([part] + fetch(part, "col", X))
    ha, hb = sweep(product, h_start, "samp", 64, (part, swap(part)), 2)

    row_a, row_b = join([ha] + fetch(ha, "samp", Z) + [hb] + fetch(hb, "samp", Y), 2)
    h_out = lay_h([row_a] + fetch(row_a, "samp", Y) + [row_b] + fetch(row_b, "samp", Z))
    return (w_out, h_out)


def solution(mesh):
    return jax.shard_map(
        shards,
        mesh=mesh,
        in_specs=(P("samp", "col"), P("samp", None), P("col", None)),
        out_specs=(P("samp", None), P("col", None)),
        check_vma=False,
    )
```

```python
import functools
import jax
import jax.numpy as jnp
from jax import lax
from jax.experimental import pallas as pl
from jax.experimental.pallas import tpu as pltpu
from jax.sharding import PartitionSpec as P

BLOCK = 128
SWEEPS = 3
floor_value = 1e-06
REL = (0, 1, 3, 2)
f32, bf16 = jnp.float32, jnp.bfloat16
ANY = pl.BlockSpec(memory_space=pl.ANY)
HBM = pl.BlockSpec(memory_space=pltpu.HBM)
VM = pl.BlockSpec(memory_space=pltpu.VMEM)


def sds(*shape, dtype=f32):
    return jax.ShapeDtypeStruct(shape, dtype)


def cost(flops, nbytes):
    return pl.CostEstimate(flops=flops, bytes_accessed=nbytes, transcendentals=0)


def params(mib):
    return pltpu.CompilerParams(vmem_limit_bytes=mib << 20)


def split(a):
    hi = a.astype(bf16)
    return hi, (a - hi.astype(f32)).astype(bf16)


def dot3(ah, al, bh, bl):
    d = functools.partial(jnp.dot, preferred_element_type=f32)
    return d(ah, bh) + (d(ah, bl) + d(al, bh))


def place():
    s, q = lax.axis_index("samp"), lax.axis_index("col")
    return s // 4, s % 4, q // 2, q % 2


def prod_kernel(chunks, sibling, first, recv, last, *refs):
    refs = list(refs)
    x_ref = refs.pop(0)
    if first:
        h_ref = refs.pop(0)
    else:
        hh_ref, hl_ref = refs.pop(0), refs.pop(0)
    recv_ref = refs.pop(0) if recv else None
    low_ref = refs.pop(0) if last else None
    out_ref = refs.pop(0)
    if first:
        hh_ref, hl_ref = refs.pop(0), refs.pop(0)
        hh, hl = split(h_ref[...])
        hh_ref[...] = hh
        hl_ref[...] = hl
    _, _, _, c = place()
    cc = 1 - c if sibling else c
    if last:
        tmp, sem = refs
        low = pltpu.make_async_copy(low_ref, out_ref.at[pl.ds(0, 512), :], sem.at[0])
        low.start()
    rows = [x_ref[pl.ds(pl.multiple_of(512 * k + 256 * cc, 256), 256), :] for k in chunks]
    ah, al = split(jnp.concatenate(rows, axis=0))
    out = dot3(ah, al, hh_ref[...], hl_ref[...])
    if recv:
        out = out + recv_ref[...]
    if last:
        tmp[...] = out
        high = pltpu.make_async_copy(tmp, out_ref.at[pl.ds(512, 512), :], sem.at[1])
        high.start()
        low.wait()
        high.wait()
    else:
        out_ref[...] = out


def prod(spectra, h, chunks, sibling, recv=None, low=None):
    first = not isinstance(h, tuple)
    last = low is not None
    ins = [spectra] + ([h] if first else list(h)) + ([] if recv is None else [recv]) + ([low] if last else [])
    outs = [sds(1024 if last else 512, 512)]
    if first:
        outs += [sds(1024, 512, dtype=bf16)] * 2
    out = pl.pallas_call(
        functools.partial(prod_kernel, chunks, sibling, first, recv is not None, last),
        out_shape=outs,
        in_specs=[VM] * len(ins),
        out_specs=[HBM] if last else [VM] * len(outs),
        scratch_shapes=[pltpu.VMEM((512, 512), f32), pltpu.SemaphoreType.DMA((2,))] if last else [],
        compiler_params=params(14),
        cost_estimate=cost(6 * 512 * 1024 * 512, 6 << 20),
        name="prod",
    )(*ins)
    return out if first else out[0]


def flip_kernel(x_ref, th_ref, tl_ref):
    for k in range(0, 1024, 128):
        hi, lo = split(x_ref[:, k : k + 128].T)
        th_ref[0, k : k + 128, :] = hi
        tl_ref[0, k : k + 128, :] = lo


def flip(spectra):
    spec = pl.BlockSpec((1, 1024, 128), lambda i: (i, 0, 0))
    return pl.pallas_call(
        flip_kernel,
        grid=(16,),
        out_shape=[sds(16, 1024, 128, dtype=bf16)] * 2,
        in_specs=[pl.BlockSpec((128, 1024), lambda i: (i, 0))],
        out_specs=[spec, spec],
        compiler_params=params(6),
        cost_estimate=cost(1 << 24, 16 << 20),
        name="flip",
    )(spectra)


def back_kernel(chunks, later, *refs):
    refs = list(refs)
    th_ref, tl_ref = refs.pop(0), refs.pop(0)
    ws = [refs.pop(0) for _ in chunks]
    acc_ref = refs.pop(0) if later else None
    if later:
        refs.pop(0)
    out_ref, w_out, sem = refs[:3]
    z, y, x, c = place()
    at, copies = [], []
    for k, (r, sibling) in enumerate(chunks):
        first = 2 * (2 * ((x + r) % 4) + (1 - c if sibling else c))
        at += [first, first + 1]
        cp = pltpu.make_async_copy(ws[k], w_out.at[pl.ds(pl.multiple_of(128 * first, 256), 256), :], sem.at[k])
        cp.start()
        copies.append(cp)
    wh, wl = split(jnp.concatenate([w[...] for w in ws], axis=0))
    for k in range(0, 1024, 512):
        rows = slice(k, k + 512)
        ah = jnp.concatenate([th_ref[i, rows, :] for i in at], axis=1)
        al = jnp.concatenate([tl_ref[i, rows, :] for i in at], axis=1)
        out = dot3(ah, al, wh, wl)
        if later:
            out = out + acc_ref[rows, :]
        if len(refs) > 3:
            refs[3][rows, :] = out
            cp = pltpu.make_async_copy(refs[3].at[rows, :], out_ref.at[rows, :], sem.at[2 + k // 512])
            cp.start()
            copies.append(cp)
        else:
            out_ref[rows, :] = out
    for cp in copies:
        cp.wait()


def back(flipped, ws, chunks, carry=(), last=False):
    ins = list(flipped) + list(ws) + list(carry)
    n = len(ins)
    return pl.pallas_call(
        functools.partial(back_kernel, tuple(chunks), bool(carry)),
        out_shape=[sds(1024, 512), sds(2048, 512)],
        in_specs=[VM] * (2 + len(ws)) + ([VM, HBM] if carry else []),
        out_specs=[HBM if last else VM, HBM],
        scratch_shapes=[pltpu.SemaphoreType.DMA((4,))] + ([pltpu.VMEM((1024, 512), f32)] if last else []),
        input_output_aliases={n - 1: 1} if carry else {},
        compiler_params=params(12),
        cost_estimate=cost(6 * 1024 * 512 * 256 * len(chunks), 6 << 20),
        name="back",
    )(*ins)


def gram_h_kernel(h_ref, mine_ref, theirs_ref, tmp):
    z, y, _, c = place()
    h = h_ref[...]
    tmp[...] = h.T
    left = tmp[pl.ds(pl.multiple_of(32 * (4 * z + y), 32), 32), :]
    both = dot3(*split(left), *split(h))
    first = (c == 0).astype(f32)
    mine_ref[...] = both[:16] * first + both[16:] * (1.0 - first)
    theirs_ref[...] = both[16:] * first + both[:16] * (1.0 - first)


def gram_h(h):
    return pl.pallas_call(
        gram_h_kernel,
        out_shape=[sds(16, 512)] * 2,
        in_specs=[VM],
        out_specs=[VM] * 2,
        scratch_shapes=[pltpu.VMEM((512, 1024), f32)],
        compiler_params=params(12),
        cost_estimate=cost(6 * 512 * 32 * 1024, 4 << 20),
        name="gram_h",
    )(h)


def gram_w_kernel(w_ref, mine_ref, theirs_ref, tmp):
    z, y, _, c = place()
    w = w_ref[...]
    tmp[...] = dot3(*split(w.T), *split(w))
    for k in range(4):
        for m in range(4):
            s = 4 * ((z + REL[k]) % 4) + (y + REL[m]) % 4
            at = 64 * k + 16 * m
            mine_ref[at : at + 16, :] = tmp[pl.ds(pl.multiple_of(32 * s + 16 * c, 16), 16), :]
            theirs_ref[at : at + 16, :] = tmp[pl.ds(pl.multiple_of(32 * s + 16 * (1 - c), 16), 16), :]


def gram_w(w):
    return pl.pallas_call(
        gram_w_kernel,
        out_shape=[sds(256, 512)] * 2,
        in_specs=[VM],
        out_specs=[VM] * 2,
        scratch_shapes=[pltpu.VMEM((512, 512), f32)],
        compiler_params=params(10),
        cost_estimate=cost(6 * 512 * 512 * 256, 4 << 20),
        name="gram_w",
    )(w)


def sweep_kernel(axis, product, start, mine, theirs, *refs):
    outs, (g, gh, gl, fh, fl, ff, pp, sem) = refs[:-8], refs[-8:]
    z, y, x, c = place()
    n = ff.shape[0]
    if axis == "col":
        rows = start
    else:
        rows = start.at[pl.ds(pl.multiple_of(n * (4 * z + y), n), n), :]
    begin = pltpu.make_async_copy(rows, ff, sem)
    begin.start()
    for t, piece in enumerate((mine, theirs)):
        cc = c if t == 0 else 1 - c
        for j in range(4):
            for i in range(4):
                row = 32 * (4 * ((z + REL[i]) % 4) + (y + REL[j]) % 4) + 16 * cc
                g[pl.ds(pl.multiple_of(row, 16), 16), :] = piece[64 * j + 16 * i : 64 * j + 16 * i + 16, :]
    hi, lo = split(g[...])
    gh[...] = hi
    gl[...] = lo
    inv = []
    for b in range(0, 512, BLOCK):
        inv.append(1.0 / jnp.sum(g[b : b + BLOCK, b : b + BLOCK], axis=0, keepdims=True))
    total = product[:n, :]
    for k in range(n, product.shape[0], n):
        total = total + product[k : k + n, :]
    pp[...] = total
    begin.wait()
    hi, lo = split(ff[...])
    fh[...] = hi
    fl[...] = lo
    for _ in range(SWEEPS):
        for k, b in enumerate(range(0, 512, BLOCK)):
            cols = slice(b, b + BLOCK)
            fg = dot3(fh[...], fl[...], gh[:, cols], gl[:, cols])
            new = jnp.maximum(ff[:, cols] + (pp[:, cols] - fg) * inv[k], floor_value)
            ff[:, cols] = new
            hi, lo = split(new)
            fh[:, cols] = hi
            fl[:, cols] = lo
    n = n // len(outs)
    for k, out in enumerate(outs):
        out[...] = ff[n * k : n * (k + 1), :]


def sweep(product, start, axis, rows, pieces, nout):
    return pl.pallas_call(
        functools.partial(sweep_kernel, axis),
        out_shape=[sds(rows // nout, 512)] * nout,
        in_specs=[VM, VM if axis == "col" else HBM, VM, VM],
        out_specs=[VM] * nout,
        scratch_shapes=[
            pltpu.VMEM((512, 512), f32),
            pltpu.VMEM((512, 512), bf16),
            pltpu.VMEM((512, 512), bf16),
            pltpu.VMEM((rows, 512), bf16),
            pltpu.VMEM((rows, 512), bf16),
            pltpu.VMEM((rows, 512), f32),
            pltpu.VMEM((rows, 512), f32),
            pltpu.SemaphoreType.DMA,
        ],
        compiler_params=params(12 if axis == "col" else 50),
        cost_estimate=cost(72 * rows * 512 * 512, 4 << 20),
        name="sweep",
    )(product, start, *pieces)


def take_kernel(w_ref, out_ref, sem):
    _, _, x, c = place()
    rows = w_ref.at[pl.ds(pl.multiple_of(256 * (2 * x + c), 256), 256), :]
    cp = pltpu.make_async_copy(rows, out_ref, sem)
    cp.start()
    cp.wait()


def take(w_start):
    return pl.pallas_call(
        take_kernel,
        out_shape=sds(256, 512),
        in_specs=[HBM],
        out_specs=VM,
        scratch_shapes=[pltpu.SemaphoreType.DMA],
        compiler_params=params(57),
        cost_estimate=cost(0, 1 << 20),
        name="take",
    )(w_start)


def lay_h_kernel(*refs):
    ins, out = refs[:8], refs[8]
    z, y, _, _ = place()
    for half in range(2):
        for j in range(4):
            for i in range(4):
                dz, dy = (REL[i], REL[j]) if half == 0 else (REL[j], REL[i])
                row = pl.multiple_of(64 * (4 * ((z + dz) % 4) + (y + dy) % 4) + 32 * half, 32)
                out[pl.ds(row, 32), :] = ins[4 * half + j][32 * i : 32 * (i + 1), :]


def lay_h(pieces):
    return pl.pallas_call(
        lay_h_kernel,
        out_shape=sds(1024, 512),
        in_specs=[VM] * 8,
        out_specs=VM,
        compiler_params=params(6),
        cost_estimate=cost(0, 4 << 20),
        name="lay_h",
    )(*pieces)


def moves(axis, dim):
    out = {}
    for r in range(4):
        pairs = []
        if axis == "col":
            for i in range(8):
                x, c = i // 2, i % 2
                pairs.append((i, 2 * x + 1 - c) if dim == "core" else (i, 2 * ((x + r) % 4) + c))
        else:
            for i in range(16):
                z, y = i // 4, i % 4
                pairs.append((i, 4 * ((z + r) % 4) + y) if dim == "z" else (i, 4 * z + (y + r) % 4))
        out[r] = pairs
    return out


XGROUPS = [[0, 2, 4, 6], [1, 3, 5, 7]]
CORE, X = moves("col", "core"), moves("col", "x")
Y, Z = moves("samp", "y"), moves("samp", "z")


def swap(a):
    return lax.ppermute(a, "col", CORE[0])


def send(a, axis, table, r):
    return lax.ppermute(a, axis, table[r])


def fetch(a, axis, table):
    return [lax.ppermute(a, axis, table[(4 - r) % 4]) for r in REL[1:]]


def after(a, *others):
    return lax.optimization_barrier((a,) + others)[0]


def join_kernel(nout, *refs):
    ins, outs = refs[:-nout], refs[-nout:]
    n = len(ins) // nout
    for k, out in enumerate(outs):
        rows = ins[n * k].shape[0]
        for i in range(n):
            out[rows * i : rows * (i + 1), :] = ins[n * k + i][...]


def join(parts, nout=1):
    rows = parts[0].shape[0] * len(parts) // nout
    out = pl.pallas_call(
        functools.partial(join_kernel, nout),
        out_shape=[sds(rows, 512)] * nout,
        in_specs=[VM] * len(parts),
        out_specs=[VM] * nout,
        compiler_params=params(4),
        cost_estimate=cost(0, rows * nout * 4096),
        name="join",
    )(*parts)
    return out if nout > 1 else out[0]


def add_kernel(n, *refs):
    total = refs[0][...]
    for r in refs[1:n]:
        total = total + r[...]
    outs = refs[n:]
    rows = total.shape[0] // len(outs)
    for k, out in enumerate(outs):
        out[...] = total[rows * k : rows * (k + 1)]


def add(parts, nout=1):
    rows = parts[0].shape[0]
    out = pl.pallas_call(
        functools.partial(add_kernel, len(parts)),
        out_shape=[sds(rows // nout, 512)] * nout,
        in_specs=[VM] * len(parts),
        out_specs=[VM] * nout,
        compiler_params=params(4),
        cost_estimate=cost(rows * 512 * len(parts), rows * 4096 * len(parts)),
        name="add",
    )(*parts)
    return out if nout > 1 else out[0]


def deal(pieces, axis, table):
    return [pieces[0]] + [send(pieces[k], axis, table, REL[k]) for k in (1, 2, 3)]


def spread(strip):
    strip = join([strip] + fetch(strip, "samp", Z))
    return join([strip] + fetch(strip, "samp", Y))


def shards(spectra, w_start, h_start):
    g_mine, g_theirs = gram_h(h_start)
    strip = add([g_mine, swap(g_theirs)])

    a1, hh, hl = prod(spectra, after(h_start, strip), (0, 1), True)
    r1 = swap(a1)
    strip = add([after(strip, a1)] + fetch(strip, "col", X))
    h = (after(hh, strip), hl)
    a2 = prod(spectra, h, (2, 3), True)
    r2 = swap(a2)
    low = prod(spectra, h, (0, 1), False, after(r1, a2))
    both = prod(spectra, h, (2, 3), False, r2, low)
    product = lax.all_to_all(both, "col", 0, 0, axis_index_groups=XGROUPS, tiled=True)

    part = spread(after(strip, both))
    w0 = take(after(w_start, part))
    (w,) = sweep(product, w0, "col", 256, (part, swap(part)), 1)

    ws = swap(w)
    near_p, near_m = send(w, "col", X, 3), send(w, "col", X, 1)

    g_mine, g_theirs = gram_w(w)
    flipped = flip(after(spectra, g_theirs))
    strips = add([g_mine, after(swap(g_theirs), *flipped)], 4)
    strips = deal(strips, "samp", Z)
    carry = back(flipped, (w, ws), ((0, False), (0, True)))
    strips = add([after(strips[0], carry[0])] + strips[1:], 4)
    near_p, near_m = after(near_p, *strips), after(near_m, *strips)
    far = send(after(w, near_p, near_m), "col", X, 2)
    sib_p, sib_m = swap(near_p), swap(near_m)
    strips = deal(strips, "samp", Y)
    carry = back(flipped, (near_p, near_m), ((1, False), (3, False)), (after(carry[0], *strips), carry[1]))
    strip = add([after(strips[0], carry[0])] + strips[1:])
    carry = back(flipped, (sib_p, sib_m), ((1, True), (3, True)), (after(carry[0], strip), carry[1]))
    part = join([after(strip, carry[0])] + fetch(strip, "samp", Z))
    sib_f = swap(after(far, part))
    carry = (after(carry[0], part), carry[1])
    back_sum, w_out = back(flipped, (far, sib_f), ((2, False), (2, True)), carry, True)

    product = lax.all_to_all(back_sum, "samp", 0, 0, tiled=True)
    part = after(part, back_sum)
    part = add([part] + fetch(part, "col", X))
    part = join([part] + fetch(part, "samp", Y))
    ha, hb = sweep(product, h_start, "samp", 64, (part, swap(part)), 2)

    row_a, row_b = join([ha] + fetch(ha, "samp", Z) + [hb] + fetch(hb, "samp", Y), 2)
    h_out = lay_h([row_a] + fetch(row_a, "samp", Y) + [row_b] + fetch(row_b, "samp", Z))
    return (w_out, h_out)


def solution(mesh):
    return jax.shard_map(
        shards,
        mesh=mesh,
        in_specs=(P("samp", "col"), P("samp", None), P("col", None)),
        out_specs=(P("samp", None), P("col", None)),
        check_vma=False,
    )
```

```python
import functools
import jax
import jax.numpy as jnp
from jax import lax
from jax.experimental import pallas as pl
from jax.experimental.pallas import tpu as pltpu
from jax.sharding import PartitionSpec as P

BLOCK = 128
SWEEPS = 3
floor_value = 1e-06
REL = (0, 1, 3, 2)
f32, bf16 = jnp.float32, jnp.bfloat16
ANY = pl.BlockSpec(memory_space=pl.ANY)
HBM = pl.BlockSpec(memory_space=pltpu.HBM)
VM = pl.BlockSpec(memory_space=pltpu.VMEM)


def sds(*shape, dtype=f32):
    return jax.ShapeDtypeStruct(shape, dtype)


def cost(flops, nbytes):
    return pl.CostEstimate(flops=flops, bytes_accessed=nbytes, transcendentals=0)


def params(mib):
    return pltpu.CompilerParams(vmem_limit_bytes=mib << 20)


def split(a):
    hi = a.astype(bf16)
    return hi, (a - hi.astype(f32)).astype(bf16)


def dot3(ah, al, bh, bl):
    d = functools.partial(jnp.dot, preferred_element_type=f32)
    return d(ah, bh) + (d(ah, bl) + d(al, bh))


def place():
    s, q = lax.axis_index("samp"), lax.axis_index("col")
    return s // 4, s % 4, q // 2, q % 2


def prod_kernel(chunks, sibling, first, recv, last, *refs):
    refs = list(refs)
    x_ref = refs.pop(0)
    if first:
        h_ref = refs.pop(0)
    else:
        hh_ref, hl_ref = refs.pop(0), refs.pop(0)
    recv_ref = refs.pop(0) if recv else None
    low_ref = refs.pop(0) if last else None
    out_ref = refs.pop(0)
    if first:
        hh_ref, hl_ref = refs.pop(0), refs.pop(0)
        hh, hl = split(h_ref[...])
        hh_ref[...] = hh
        hl_ref[...] = hl
    _, _, _, c = place()
    cc = 1 - c if sibling else c
    if last:
        tmp, sem = refs
        low = pltpu.make_async_copy(low_ref, out_ref.at[pl.ds(0, 512), :], sem.at[0])
        low.start()
    rows = [x_ref[pl.ds(pl.multiple_of(512 * k + 256 * cc, 256), 256), :] for k in chunks]
    ah, al = split(jnp.concatenate(rows, axis=0))
    out = dot3(ah, al, hh_ref[...], hl_ref[...])
    if recv:
        out = out + recv_ref[...]
    if last:
        tmp[...] = out
        high = pltpu.make_async_copy(tmp, out_ref.at[pl.ds(512, 512), :], sem.at[1])
        high.start()
        low.wait()
        high.wait()
    else:
        out_ref[...] = out


def prod(spectra, h, chunks, sibling, recv=None, low=None):
    first = not isinstance(h, tuple)
    last = low is not None
    ins = [spectra] + ([h] if first else list(h)) + ([] if recv is None else [recv]) + ([low] if last else [])
    outs = [sds(1024 if last else 512, 512)]
    if first:
        outs += [sds(1024, 512, dtype=bf16)] * 2
    out = pl.pallas_call(
        functools.partial(prod_kernel, chunks, sibling, first, recv is not None, last),
        out_shape=outs,
        in_specs=[VM] * len(ins),
        out_specs=[HBM] if last else [VM] * len(outs),
        scratch_shapes=[pltpu.VMEM((512, 512), f32), pltpu.SemaphoreType.DMA((2,))] if last else [],
        compiler_params=params(14),
        cost_estimate=cost(6 * 512 * 1024 * 512, 6 << 20),
        name="prod",
    )(*ins)
    return out if first else out[0]


def flip_kernel(x_ref, th_ref, tl_ref):
    for k in range(0, 1024, 128):
        hi, lo = split(x_ref[:, k : k + 128].T)
        th_ref[0, k : k + 128, :] = hi
        tl_ref[0, k : k + 128, :] = lo


def flip(spectra):
    spec = pl.BlockSpec((1, 1024, 128), lambda i: (i, 0, 0))
    return pl.pallas_call(
        flip_kernel,
        grid=(16,),
        out_shape=[sds(16, 1024, 128, dtype=bf16)] * 2,
        in_specs=[pl.BlockSpec((128, 1024), lambda i: (i, 0))],
        out_specs=[spec, spec],
        compiler_params=params(6),
        cost_estimate=cost(1 << 24, 16 << 20),
        name="flip",
    )(spectra)


def back_kernel(chunks, later, *refs):
    refs = list(refs)
    th_ref, tl_ref = refs.pop(0), refs.pop(0)
    ws = [refs.pop(0) for _ in chunks]
    acc_ref = refs.pop(0) if later else None
    if later:
        refs.pop(0)
    out_ref, w_out, sem = refs[:3]
    z, y, x, c = place()
    at, copies = [], []
    for k, (r, sibling) in enumerate(chunks):
        first = 2 * (2 * ((x + r) % 4) + (1 - c if sibling else c))
        at += [first, first + 1]
        cp = pltpu.make_async_copy(ws[k], w_out.at[pl.ds(pl.multiple_of(128 * first, 256), 256), :], sem.at[k])
        cp.start()
        copies.append(cp)
    wh, wl = split(jnp.concatenate([w[...] for w in ws], axis=0))
    for k in range(0, 1024, 512):
        rows = slice(k, k + 512)
        ah = jnp.concatenate([th_ref[i, rows, :] for i in at], axis=1)
        al = jnp.concatenate([tl_ref[i, rows, :] for i in at], axis=1)
        out = dot3(ah, al, wh, wl)
        if later:
            out = out + acc_ref[rows, :]
        if len(refs) > 3:
            refs[3][rows, :] = out
            cp = pltpu.make_async_copy(refs[3].at[rows, :], out_ref.at[rows, :], sem.at[2 + k // 512])
            cp.start()
            copies.append(cp)
        else:
            out_ref[rows, :] = out
    for cp in copies:
        cp.wait()


def back(flipped, ws, chunks, carry=(), last=False):
    ins = list(flipped) + list(ws) + list(carry)
    n = len(ins)
    return pl.pallas_call(
        functools.partial(back_kernel, tuple(chunks), bool(carry)),
        out_shape=[sds(1024, 512), sds(2048, 512)],
        in_specs=[VM] * (2 + len(ws)) + ([VM, HBM] if carry else []),
        out_specs=[HBM if last else VM, HBM],
        scratch_shapes=[pltpu.SemaphoreType.DMA((4,))] + ([pltpu.VMEM((1024, 512), f32)] if last else []),
        input_output_aliases={n - 1: 1} if carry else {},
        compiler_params=params(12),
        cost_estimate=cost(6 * 1024 * 512 * 256 * len(chunks), 6 << 20),
        name="back",
    )(*ins)


def gram_h_kernel(h_ref, mine_ref, theirs_ref, tmp):
    z, y, _, c = place()
    h = h_ref[...]
    tmp[...] = h.T
    left = tmp[pl.ds(pl.multiple_of(32 * (4 * z + y), 32), 32), :]
    both = dot3(*split(left), *split(h))
    first = (c == 0).astype(f32)
    mine_ref[...] = both[:16] * first + both[16:] * (1.0 - first)
    theirs_ref[...] = both[16:] * first + both[:16] * (1.0 - first)


def gram_h(h):
    return pl.pallas_call(
        gram_h_kernel,
        out_shape=[sds(16, 512)] * 2,
        in_specs=[VM],
        out_specs=[VM] * 2,
        scratch_shapes=[pltpu.VMEM((512, 1024), f32)],
        compiler_params=params(12),
        cost_estimate=cost(6 * 512 * 32 * 1024, 4 << 20),
        name="gram_h",
    )(h)


def gram_w_kernel(w_ref, mine_ref, theirs_ref, tmp):
    _, _, _, c = place()
    w = w_ref[...]
    tmp[...] = dot3(*split(w.T), *split(w))
    for s in range(16):
        rows = slice(16 * s, 16 * s + 16)
        mine_ref[rows, :] = tmp[pl.ds(pl.multiple_of(32 * s + 16 * c, 16), 16), :]
        theirs_ref[rows, :] = tmp[pl.ds(pl.multiple_of(32 * s + 16 * (1 - c), 16), 16), :]


def gram_w(w):
    return pl.pallas_call(
        gram_w_kernel,
        out_shape=[sds(256, 512)] * 2,
        in_specs=[VM],
        out_specs=[VM] * 2,
        scratch_shapes=[pltpu.VMEM((512, 512), f32)],
        compiler_params=params(10),
        cost_estimate=cost(6 * 512 * 512 * 256, 4 << 20),
        name="gram_w",
    )(w)


def sweep_kernel(axis, product, start, mine, theirs, *refs):
    outs, (g, gh, gl, fh, fl, ff, pp, sem) = refs[:-8], refs[-8:]
    z, y, x, c = place()
    n = ff.shape[0]
    if axis == "col":
        rows = start
    else:
        rows = start.at[pl.ds(pl.multiple_of(n * (4 * z + y), n), n), :]
    begin = pltpu.make_async_copy(rows, ff, sem)
    begin.start()
    for t, piece in enumerate((mine, theirs)):
        cc = c if t == 0 else 1 - c
        for j in range(4):
            for i in range(4):
                row = 32 * (4 * ((z + REL[i]) % 4) + (y + REL[j]) % 4) + 16 * cc
                g[pl.ds(pl.multiple_of(row, 16), 16), :] = piece[64 * j + 16 * i : 64 * j + 16 * i + 16, :]
    hi, lo = split(g[...])
    gh[...] = hi
    gl[...] = lo
    inv = []
    for b in range(0, 512, BLOCK):
        inv.append(1.0 / jnp.sum(g[b : b + BLOCK, b : b + BLOCK], axis=0, keepdims=True))
    total = product[:n, :]
    for k in range(n, product.shape[0], n):
        total = total + product[k : k + n, :]
    pp[...] = total
    begin.wait()
    hi, lo = split(ff[...])
    fh[...] = hi
    fl[...] = lo
    for _ in range(SWEEPS):
        for k, b in enumerate(range(0, 512, BLOCK)):
            cols = slice(b, b + BLOCK)
            fg = dot3(fh[...], fl[...], gh[:, cols], gl[:, cols])
            new = jnp.maximum(ff[:, cols] + (pp[:, cols] - fg) * inv[k], floor_value)
            ff[:, cols] = new
            hi, lo = split(new)
            fh[:, cols] = hi
            fl[:, cols] = lo
    n = n // len(outs)
    for k, out in enumerate(outs):
        out[...] = ff[n * k : n * (k + 1), :]


def sweep(product, start, axis, rows, pieces, nout):
    return pl.pallas_call(
        functools.partial(sweep_kernel, axis),
        out_shape=[sds(rows // nout, 512)] * nout,
        in_specs=[VM, VM if axis == "col" else HBM, VM, VM],
        out_specs=[VM] * nout,
        scratch_shapes=[
            pltpu.VMEM((512, 512), f32),
            pltpu.VMEM((512, 512), bf16),
            pltpu.VMEM((512, 512), bf16),
            pltpu.VMEM((rows, 512), bf16),
            pltpu.VMEM((rows, 512), bf16),
            pltpu.VMEM((rows, 512), f32),
            pltpu.VMEM((rows, 512), f32),
            pltpu.SemaphoreType.DMA,
        ],
        compiler_params=params(12 if axis == "col" else 50),
        cost_estimate=cost(72 * rows * 512 * 512, 4 << 20),
        name="sweep",
    )(product, start, *pieces)


def take_kernel(w_ref, out_ref, sem):
    _, _, x, c = place()
    rows = w_ref.at[pl.ds(pl.multiple_of(256 * (2 * x + c), 256), 256), :]
    cp = pltpu.make_async_copy(rows, out_ref, sem)
    cp.start()
    cp.wait()


def take(w_start):
    return pl.pallas_call(
        take_kernel,
        out_shape=sds(256, 512),
        in_specs=[HBM],
        out_specs=VM,
        scratch_shapes=[pltpu.SemaphoreType.DMA],
        compiler_params=params(57),
        cost_estimate=cost(0, 1 << 20),
        name="take",
    )(w_start)


def lay_h_kernel(*refs):
    ins, out = refs[:8], refs[8]
    z, y, _, _ = place()
    for half in range(2):
        for j in range(4):
            for i in range(4):
                dz, dy = (REL[i], REL[j]) if half == 0 else (REL[j], REL[i])
                row = pl.multiple_of(64 * (4 * ((z + dz) % 4) + (y + dy) % 4) + 32 * half, 32)
                out[pl.ds(row, 32), :] = ins[4 * half + j][32 * i : 32 * (i + 1), :]


def lay_h(pieces):
    return pl.pallas_call(
        lay_h_kernel,
        out_shape=sds(1024, 512),
        in_specs=[VM] * 8,
        out_specs=VM,
        compiler_params=params(6),
        cost_estimate=cost(0, 4 << 20),
        name="lay_h",
    )(*pieces)


def moves(axis, dim):
    out = {}
    for r in range(4):
        pairs = []
        if axis == "col":
            for i in range(8):
                x, c = i // 2, i % 2
                pairs.append((i, 2 * x + 1 - c) if dim == "core" else (i, 2 * ((x + r) % 4) + c))
        else:
            for i in range(16):
                z, y = i // 4, i % 4
                pairs.append((i, 4 * ((z + r) % 4) + y) if dim == "z" else (i, 4 * z + (y + r) % 4))
        out[r] = pairs
    return out


XGROUPS = [[0, 2, 4, 6], [1, 3, 5, 7]]
CORE, X = moves("col", "core"), moves("col", "x")
Y, Z = moves("samp", "y"), moves("samp", "z")


def swap(a):
    return lax.ppermute(a, "col", CORE[0])


def send(a, axis, table, r):
    return lax.ppermute(a, axis, table[r])


def fetch(a, axis, table):
    return [lax.ppermute(a, axis, table[(4 - r) % 4]) for r in REL[1:]]


def after(a, *others):
    return lax.optimization_barrier((a,) + others)[0]


def join_kernel(nout, *refs):
    ins, outs = refs[:-nout], refs[-nout:]
    n = len(ins) // nout
    for k, out in enumerate(outs):
        rows = ins[n * k].shape[0]
        for i in range(n):
            out[rows * i : rows * (i + 1), :] = ins[n * k + i][...]


def join(parts, nout=1):
    rows = parts[0].shape[0] * len(parts) // nout
    out = pl.pallas_call(
        functools.partial(join_kernel, nout),
        out_shape=[sds(rows, 512)] * nout,
        in_specs=[VM] * len(parts),
        out_specs=[VM] * nout,
        compiler_params=params(4),
        cost_estimate=cost(0, rows * nout * 4096),
        name="join",
    )(*parts)
    return out if nout > 1 else out[0]


def add_kernel(n, *refs):
    total = refs[0][...]
    for r in refs[1:n]:
        total = total + r[...]
    refs[-1][...] = total


def add(parts, hold=None):
    rows = parts[0].shape[0]
    held = [] if hold is None else [hold]
    return pl.pallas_call(
        functools.partial(add_kernel, len(parts)),
        out_shape=sds(rows, 512),
        in_specs=[VM] * (len(parts) + len(held)),
        out_specs=VM,
        compiler_params=params(14 if held else 4),
        cost_estimate=cost(rows * 512 * len(parts), rows * 4096 * len(parts)),
        name="add",
    )(*parts, *held)


def fold_kernel(a_ref, out_ref):
    total = a_ref[:16, :]
    for k in range(16, 256, 16):
        total = total + a_ref[k : k + 16, :]
    out_ref[...] = total


def fold(a):
    return pl.pallas_call(
        fold_kernel,
        out_shape=sds(16, 512),
        in_specs=[VM],
        out_specs=VM,
        compiler_params=params(4),
        cost_estimate=cost(1 << 17, 1 << 20),
        name="fold",
    )(a)


def spread(strip):
    strip = join([strip] + fetch(strip, "samp", Z))
    return join([strip] + fetch(strip, "samp", Y))


def shards(spectra, w_start, h_start):
    g_mine, g_theirs = gram_h(h_start)
    strip = add([g_mine, swap(g_theirs)], spectra)

    a1, hh, hl = prod(spectra, after(h_start, strip), (0, 1), True)
    r1 = swap(a1)
    strip = add([after(strip, a1)] + fetch(strip, "col", X))
    h = (after(hh, strip), hl)
    a2 = prod(spectra, h, (2, 3), True)
    r2 = swap(a2)
    low = prod(spectra, h, (0, 1), False, after(r1, a2))
    both = prod(spectra, h, (2, 3), False, r2, low)
    product = lax.all_to_all(both, "col", 0, 0, axis_index_groups=XGROUPS, tiled=True)

    part = spread(after(strip, both))
    w0 = take(after(w_start, part))
    (w,) = sweep(product, w0, "col", 256, (part, swap(part)), 1)

    ws = swap(w)
    near_p, near_m = send(w, "col", X, 3), send(w, "col", X, 1)

    g_mine, g_theirs = gram_w(w)
    strip = fold(lax.all_to_all(add([g_mine, swap(g_theirs)]), "samp", 0, 0, tiled=True))
    near_p, near_m = after(near_p, strip), after(near_m, strip)
    far = send(after(w, near_p, near_m), "col", X, 2)
    sib_p, sib_m = swap(near_p), swap(near_m)
    flipped = flip(after(spectra, strip))
    carry = back(flipped, (w, ws), ((0, False), (0, True)))
    part = join([after(strip, carry[0])] + fetch(strip, "samp", Z))
    carry = back(flipped, (near_p, near_m), ((1, False), (3, False)), (after(carry[0], part), carry[1]))
    carry = back(flipped, (sib_p, sib_m), ((1, True), (3, True)), carry)
    part = join([after(part, carry[0])] + fetch(part, "samp", Y))
    sib_f = swap(after(far, part))
    carry = (after(carry[0], part), carry[1])
    back_sum, w_out = back(flipped, (far, sib_f), ((2, False), (2, True)), carry, True)

    product = lax.all_to_all(back_sum, "samp", 0, 0, tiled=True)
    part = after(part, back_sum)
    part = add([part] + fetch(part, "col", X))
    ha, hb = sweep(product, h_start, "samp", 64, (part, swap(part)), 2)

    row_a, row_b = join([ha] + fetch(ha, "samp", Z) + [hb] + fetch(hb, "samp", Y), 2)
    h_out = lay_h([row_a] + fetch(row_a, "samp", Y) + [row_b] + fetch(row_b, "samp", Z))
    return (w_out, h_out)


def solution(mesh):
    return jax.shard_map(
        shards,
        mesh=mesh,
        in_specs=(P("samp", "col"), P("samp", None), P("col", None)),
        out_specs=(P("samp", None), P("col", None)),
        check_vma=False,
    )
```

```python
import functools
import jax
import jax.numpy as jnp
from jax import lax
from jax.experimental import pallas as pl
from jax.experimental.pallas import tpu as pltpu
from jax.sharding import PartitionSpec as P

BLOCK = 128
SWEEPS = 3
floor_value = 1e-06
REL = (0, 1, 3, 2)
f32, bf16 = jnp.float32, jnp.bfloat16
ANY = pl.BlockSpec(memory_space=pl.ANY)
HBM = pl.BlockSpec(memory_space=pltpu.HBM)
VM = pl.BlockSpec(memory_space=pltpu.VMEM)


def sds(*shape, dtype=f32):
    return jax.ShapeDtypeStruct(shape, dtype)


def cost(flops, nbytes):
    return pl.CostEstimate(flops=flops, bytes_accessed=nbytes, transcendentals=0)


def params(mib):
    return pltpu.CompilerParams(vmem_limit_bytes=mib << 20)


def split(a):
    hi = a.astype(bf16)
    return hi, (a - hi.astype(f32)).astype(bf16)


def dot3(ah, al, bh, bl):
    d = functools.partial(jnp.dot, preferred_element_type=f32)
    return d(ah, bh) + (d(ah, bl) + d(al, bh))


def place():
    s, q = lax.axis_index("samp"), lax.axis_index("col")
    return s // 4, s % 4, q // 2, q % 2


def prod_kernel(chunks, sibling, first, recv, last, *refs):
    refs = list(refs)
    x_ref = refs.pop(0)
    if first:
        h_ref = refs.pop(0)
    else:
        hh_ref, hl_ref = refs.pop(0), refs.pop(0)
    recv_ref = refs.pop(0) if recv else None
    low_ref = refs.pop(0) if last else None
    out_ref = refs.pop(0)
    if first:
        hh_ref, hl_ref = refs.pop(0), refs.pop(0)
        hh, hl = split(h_ref[...])
        hh_ref[...] = hh
        hl_ref[...] = hl
    _, _, _, c = place()
    cc = 1 - c if sibling else c
    if last:
        tmp, sem = refs
        low = pltpu.make_async_copy(low_ref, out_ref.at[pl.ds(0, 512), :], sem.at[0])
        low.start()
    rows = [x_ref[pl.ds(pl.multiple_of(512 * k + 256 * cc, 256), 256), :] for k in chunks]
    ah, al = split(jnp.concatenate(rows, axis=0))
    out = dot3(ah, al, hh_ref[...], hl_ref[...])
    if recv:
        out = out + recv_ref[...]
    if last:
        tmp[...] = out
        high = pltpu.make_async_copy(tmp, out_ref.at[pl.ds(512, 512), :], sem.at[1])
        high.start()
        low.wait()
        high.wait()
    else:
        out_ref[...] = out


def prod(spectra, h, chunks, sibling, recv=None, low=None):
    first = not isinstance(h, tuple)
    last = low is not None
    ins = [spectra] + ([h] if first else list(h)) + ([] if recv is None else [recv]) + ([low] if last else [])
    outs = [sds(1024 if last else 512, 512)]
    if first:
        outs += [sds(1024, 512, dtype=bf16)] * 2
    out = pl.pallas_call(
        functools.partial(prod_kernel, chunks, sibling, first, recv is not None, last),
        out_shape=outs,
        in_specs=[VM] * len(ins),
        out_specs=[HBM] if last else [VM] * len(outs),
        scratch_shapes=[pltpu.VMEM((512, 512), f32), pltpu.SemaphoreType.DMA((2,))] if last else [],
        compiler_params=params(14),
        cost_estimate=cost(6 * 512 * 1024 * 512, 6 << 20),
        name="prod",
    )(*ins)
    return out if first else out[0]


def flip_kernel(x_ref, th_ref, tl_ref):
    for k in range(0, 1024, 128):
        hi, lo = split(x_ref[:, k : k + 128].T)
        th_ref[0, k : k + 128, :] = hi
        tl_ref[0, k : k + 128, :] = lo


def flip(spectra):
    spec = pl.BlockSpec((1, 1024, 128), lambda i: (i, 0, 0))
    return pl.pallas_call(
        flip_kernel,
        grid=(16,),
        out_shape=[sds(16, 1024, 128, dtype=bf16)] * 2,
        in_specs=[pl.BlockSpec((128, 1024), lambda i: (i, 0))],
        out_specs=[spec, spec],
        compiler_params=params(6),
        cost_estimate=cost(1 << 24, 16 << 20),
        name="flip",
    )(spectra)


def back_kernel(chunks, later, *refs):
    refs = list(refs)
    th_ref, tl_ref = refs.pop(0), refs.pop(0)
    ws = [refs.pop(0) for _ in chunks]
    acc_ref = refs.pop(0) if later else None
    if later:
        refs.pop(0)
    out_ref, w_out, sem = refs[:3]
    z, y, x, c = place()
    at, copies = [], []
    for k, (r, sibling) in enumerate(chunks):
        first = 2 * (2 * ((x + r) % 4) + (1 - c if sibling else c))
        at += [first, first + 1]
        cp = pltpu.make_async_copy(ws[k], w_out.at[pl.ds(pl.multiple_of(128 * first, 256), 256), :], sem.at[k])
        cp.start()
        copies.append(cp)
    wh, wl = split(jnp.concatenate([w[...] for w in ws], axis=0))
    for k in range(0, 1024, 512):
        rows = slice(k, k + 512)
        ah = jnp.concatenate([th_ref[i, rows, :] for i in at], axis=1)
        al = jnp.concatenate([tl_ref[i, rows, :] for i in at], axis=1)
        out = dot3(ah, al, wh, wl)
        if later:
            out = out + acc_ref[rows, :]
        if len(refs) > 3:
            refs[3][rows, :] = out
            cp = pltpu.make_async_copy(refs[3].at[rows, :], out_ref.at[rows, :], sem.at[2 + k // 512])
            cp.start()
            copies.append(cp)
        else:
            out_ref[rows, :] = out
    for cp in copies:
        cp.wait()


def back(flipped, ws, chunks, carry=(), last=False):
    ins = list(flipped) + list(ws) + list(carry)
    n = len(ins)
    return pl.pallas_call(
        functools.partial(back_kernel, tuple(chunks), bool(carry)),
        out_shape=[sds(1024, 512), sds(2048, 512)],
        in_specs=[VM] * (2 + len(ws)) + ([VM, HBM] if carry else []),
        out_specs=[HBM if last else VM, HBM],
        scratch_shapes=[pltpu.SemaphoreType.DMA((4,))] + ([pltpu.VMEM((1024, 512), f32)] if last else []),
        input_output_aliases={n - 1: 1} if carry else {},
        compiler_params=params(12),
        cost_estimate=cost(6 * 1024 * 512 * 256 * len(chunks), 6 << 20),
        name="back",
    )(*ins)


def gram_h_kernel(h_ref, _, mine_ref, theirs_ref, tmp):
    z, y, _, c = place()
    h = h_ref[...]
    tmp[...] = h.T
    left = tmp[pl.ds(pl.multiple_of(32 * (4 * z + y), 32), 32), :]
    both = dot3(*split(left), *split(h))
    first = (c == 0).astype(f32)
    mine_ref[...] = both[:16] * first + both[16:] * (1.0 - first)
    theirs_ref[...] = both[16:] * first + both[:16] * (1.0 - first)


def gram_h(h, hold):
    return pl.pallas_call(
        gram_h_kernel,
        out_shape=[sds(16, 512)] * 2,
        in_specs=[VM] * 2,
        out_specs=[VM] * 2,
        scratch_shapes=[pltpu.VMEM((512, 1024), f32)],
        compiler_params=params(14),
        cost_estimate=cost(6 * 512 * 32 * 1024, 4 << 20),
        name="gram_h",
    )(h, hold)


def gram_w_kernel(w_ref, ws_ref, *refs):
    outs, tmp = refs[:4], refs[4]
    _, _, x, c = place()
    right = jnp.concatenate([w_ref[...], ws_ref[...]], axis=0)
    tmp[...] = right.T
    rows = [tmp[pl.ds(pl.multiple_of(128 * ((x + r) % 4) + 64 * c, 64), 64), :] for r in REL]
    out = dot3(*split(jnp.concatenate(rows, axis=0)), *split(right))
    for k in range(4):
        outs[k][...] = out[64 * k : 64 * (k + 1)]


def gram_w(w, ws):
    return pl.pallas_call(
        gram_w_kernel,
        out_shape=[sds(64, 512)] * 4,
        in_specs=[VM] * 2,
        out_specs=[VM] * 4,
        scratch_shapes=[pltpu.VMEM((512, 512), f32)],
        compiler_params=params(10),
        cost_estimate=cost(6 * 256 * 512 * 512, 4 << 20),
        name="gram_w",
    )(w, ws)


def sweep_kernel(axis, product, start, mine, theirs, *refs):
    outs, (g, gh, gl, fh, fl, ff, pp, sem) = refs[:-8], refs[-8:]
    z, y, x, c = place()
    n = ff.shape[0]
    if axis == "col":
        rows = start
    else:
        rows = start.at[pl.ds(pl.multiple_of(n * (4 * z + y), n), n), :]
    begin = pltpu.make_async_copy(rows, ff, sem)
    begin.start()
    for t, piece in enumerate((mine, theirs)):
        cc = c if t == 0 else 1 - c
        for j in range(4):
            if axis == "samp":
                row = 128 * ((x + REL[j]) % 4) + 64 * cc
                g[pl.ds(pl.multiple_of(row, 64), 64), :] = piece[64 * j : 64 * j + 64, :]
                continue
            for i in range(4):
                row = 32 * (4 * ((z + REL[i]) % 4) + (y + REL[j]) % 4) + 16 * cc
                g[pl.ds(pl.multiple_of(row, 16), 16), :] = piece[64 * j + 16 * i : 64 * j + 16 * i + 16, :]
    hi, lo = split(g[...])
    gh[...] = hi
    gl[...] = lo
    inv = []
    for b in range(0, 512, BLOCK):
        inv.append(1.0 / jnp.sum(g[b : b + BLOCK, b : b + BLOCK], axis=0, keepdims=True))
    total = product[:n, :]
    for k in range(n, product.shape[0], n):
        total = total + product[k : k + n, :]
    pp[...] = total
    begin.wait()
    hi, lo = split(ff[...])
    fh[...] = hi
    fl[...] = lo
    for _ in range(SWEEPS):
        for k, b in enumerate(range(0, 512, BLOCK)):
            cols = slice(b, b + BLOCK)
            fg = dot3(fh[...], fl[...], gh[:, cols], gl[:, cols])
            new = jnp.maximum(ff[:, cols] + (pp[:, cols] - fg) * inv[k], floor_value)
            ff[:, cols] = new
            hi, lo = split(new)
            fh[:, cols] = hi
            fl[:, cols] = lo
    n = n // len(outs)
    for k, out in enumerate(outs):
        out[...] = ff[n * k : n * (k + 1), :]


def sweep(product, start, axis, rows, pieces, nout):
    return pl.pallas_call(
        functools.partial(sweep_kernel, axis),
        out_shape=[sds(rows // nout, 512)] * nout,
        in_specs=[VM, VM if axis == "col" else HBM, VM, VM],
        out_specs=[VM] * nout,
        scratch_shapes=[
            pltpu.VMEM((512, 512), f32),
            pltpu.VMEM((512, 512), bf16),
            pltpu.VMEM((512, 512), bf16),
            pltpu.VMEM((rows, 512), bf16),
            pltpu.VMEM((rows, 512), bf16),
            pltpu.VMEM((rows, 512), f32),
            pltpu.VMEM((rows, 512), f32),
            pltpu.SemaphoreType.DMA,
        ],
        compiler_params=params(12 if axis == "col" else 50),
        cost_estimate=cost(72 * rows * 512 * 512, 4 << 20),
        name="sweep",
    )(product, start, *pieces)


def take_kernel(w_ref, out_ref, sem):
    _, _, x, c = place()
    rows = w_ref.at[pl.ds(pl.multiple_of(256 * (2 * x + c), 256), 256), :]
    cp = pltpu.make_async_copy(rows, out_ref, sem)
    cp.start()
    cp.wait()


def take(w_start):
    return pl.pallas_call(
        take_kernel,
        out_shape=sds(256, 512),
        in_specs=[HBM],
        out_specs=VM,
        scratch_shapes=[pltpu.SemaphoreType.DMA],
        compiler_params=params(57),
        cost_estimate=cost(0, 1 << 20),
        name="take",
    )(w_start)


def lay_h_kernel(*refs):
    ins, out = refs[:8], refs[8]
    z, y, _, _ = place()
    for half in range(2):
        for j in range(4):
            for i in range(4):
                dz, dy = (REL[i], REL[j]) if half == 0 else (REL[j], REL[i])
                row = pl.multiple_of(64 * (4 * ((z + dz) % 4) + (y + dy) % 4) + 32 * half, 32)
                out[pl.ds(row, 32), :] = ins[4 * half + j][32 * i : 32 * (i + 1), :]


def lay_h(pieces):
    return pl.pallas_call(
        lay_h_kernel,
        out_shape=sds(1024, 512),
        in_specs=[VM] * 8,
        out_specs=VM,
        compiler_params=params(6),
        cost_estimate=cost(0, 4 << 20),
        name="lay_h",
    )(*pieces)


def moves(axis, dim):
    out = {}
    for r in range(4):
        pairs = []
        if axis == "col":
            for i in range(8):
                x, c = i // 2, i % 2
                pairs.append((i, 2 * x + 1 - c) if dim == "core" else (i, 2 * ((x + r) % 4) + c))
        else:
            for i in range(16):
                z, y = i // 4, i % 4
                pairs.append((i, 4 * ((z + r) % 4) + y) if dim == "z" else (i, 4 * z + (y + r) % 4))
        out[r] = pairs
    return out


XGROUPS = [[0, 2, 4, 6], [1, 3, 5, 7]]
CORE, X = moves("col", "core"), moves("col", "x")
Y, Z = moves("samp", "y"), moves("samp", "z")


def swap(a):
    return lax.ppermute(a, "col", CORE[0])


def send(a, axis, table, r):
    return lax.ppermute(a, axis, table[r])


def fetch(a, axis, table):
    return [lax.ppermute(a, axis, table[(4 - r) % 4]) for r in REL[1:]]


def after(a, *others):
    return lax.optimization_barrier((a,) + others)[0]


def join_kernel(nout, *refs):
    ins, outs = refs[:-nout], refs[-nout:]
    n = len(ins) // nout
    for k, out in enumerate(outs):
        rows = ins[n * k].shape[0]
        for i in range(n):
            out[rows * i : rows * (i + 1), :] = ins[n * k + i][...]


def join(parts, nout=1):
    rows = parts[0].shape[0] * len(parts) // nout
    out = pl.pallas_call(
        functools.partial(join_kernel, nout),
        out_shape=[sds(rows, 512)] * nout,
        in_specs=[VM] * len(parts),
        out_specs=[VM] * nout,
        compiler_params=params(4),
        cost_estimate=cost(0, rows * nout * 4096),
        name="join",
    )(*parts)
    return out if nout > 1 else out[0]


def add_kernel(n, *refs):
    total = refs[0][...]
    for r in refs[1:n]:
        total = total + r[...]
    refs[-1][...] = total


def add(parts):
    rows = parts[0].shape[0]
    return pl.pallas_call(
        functools.partial(add_kernel, len(parts)),
        out_shape=sds(rows, 512),
        in_specs=[VM] * len(parts),
        out_specs=VM,
        compiler_params=params(4),
        cost_estimate=cost(rows * 512 * len(parts), rows * 4096 * len(parts)),
        name="add",
    )(*parts)


def deal(pieces, axis, table):
    return [pieces[0]] + [send(pieces[k], axis, table, REL[k]) for k in (1, 2, 3)]


def spread(strip):
    strip = join([strip] + fetch(strip, "samp", Z))
    return join([strip] + fetch(strip, "samp", Y))


def shards(spectra, w_start, h_start):
    g_mine, g_theirs = gram_h(h_start, spectra)
    strip = add([g_mine, swap(g_theirs)])

    a1, hh, hl = prod(spectra, after(h_start, strip), (0, 1), True)
    r1 = swap(a1)
    strip = add([after(strip, a1)] + fetch(strip, "col", X))
    h = (after(hh, strip), hl)
    a2 = prod(spectra, h, (2, 3), True)
    r2 = swap(a2)
    low = prod(spectra, h, (0, 1), False, after(r1, a2))
    both = prod(spectra, h, (2, 3), False, r2, low)
    product = lax.all_to_all(both, "col", 0, 0, axis_index_groups=XGROUPS, tiled=True)

    part = spread(after(strip, both))
    w0 = take(after(w_start, part))
    (w,) = sweep(product, w0, "col", 256, (part, swap(part)), 1)

    ws = swap(w)
    slices = gram_w(w, ws)
    flipped = flip(after(spectra, slices[0]))
    slices = deal(slices, "col", X)
    part = add([after(slices[0], *flipped)] + slices[1:])
    late = after(w, part)
    near_p, near_m, far = send(late, "col", X, 3), send(late, "col", X, 1), send(late, "col", X, 2)
    carry = back(flipped, (w, after(ws, part)), ((0, False), (0, True)))
    part = add([after(part, carry[0])] + fetch(part, "samp", Y))
    near_p, near_m = after(near_p, part), after(near_m, part)
    sib_p, sib_m = swap(near_p), swap(near_m)
    carry = back(flipped, (near_p, near_m), ((1, False), (3, False)), carry)
    part = add([after(part, carry[0])] + fetch(part, "samp", Z))
    carry = back(flipped, (sib_p, sib_m), ((1, True), (3, True)), carry)
    sib_f = swap(after(far, part))
    carry = (after(carry[0], part), carry[1])
    back_sum, w_out = back(flipped, (far, sib_f), ((2, False), (2, True)), carry, True)

    product = lax.all_to_all(back_sum, "samp", 0, 0, tiled=True)
    part = after(part, back_sum)
    part = join([part] + fetch(part, "col", X))
    ha, hb = sweep(product, h_start, "samp", 64, (part, swap(part)), 2)

    row_a, row_b = join([ha] + fetch(ha, "samp", Z) + [hb] + fetch(hb, "samp", Y), 2)
    h_out = lay_h([row_a] + fetch(row_a, "samp", Y) + [row_b] + fetch(row_b, "samp", Z))
    return (w_out, h_out)


def solution(mesh):
    return jax.shard_map(
        shards,
        mesh=mesh,
        in_specs=(P("samp", "col"), P("samp", None), P("col", None)),
        out_specs=(P("samp", None), P("col", None)),
        check_vma=False,
    )
```

```python
import functools
import jax
import jax.numpy as jnp
from jax import lax
from jax.experimental import pallas as pl
from jax.experimental.pallas import tpu as pltpu
from jax.sharding import PartitionSpec as P

BLOCK = 128
SWEEPS = 3
floor_value = 1e-06
REL = (0, 1, 3, 2)
f32, bf16 = jnp.float32, jnp.bfloat16
ANY = pl.BlockSpec(memory_space=pl.ANY)
HBM = pl.BlockSpec(memory_space=pltpu.HBM)
VM = pl.BlockSpec(memory_space=pltpu.VMEM)


def sds(*shape, dtype=f32):
    return jax.ShapeDtypeStruct(shape, dtype)


def cost(flops, nbytes):
    return pl.CostEstimate(flops=flops, bytes_accessed=nbytes, transcendentals=0)


def params(mib):
    return pltpu.CompilerParams(vmem_limit_bytes=mib << 20)


def split(a):
    hi = a.astype(bf16)
    return hi, (a - hi.astype(f32)).astype(bf16)


def dot3(ah, al, bh, bl):
    d = functools.partial(jnp.dot, preferred_element_type=f32)
    return d(ah, bh) + (d(ah, bl) + d(al, bh))


def place():
    s, q = lax.axis_index("samp"), lax.axis_index("col")
    return s // 4, s % 4, q // 2, q % 2


def prod_kernel(chunks, sibling, first, recv, last, *refs):
    refs = list(refs)
    x_ref = refs.pop(0)
    if first:
        h_ref = refs.pop(0)
    else:
        hh_ref, hl_ref = refs.pop(0), refs.pop(0)
    recv_ref = refs.pop(0) if recv else None
    low_ref = refs.pop(0) if last else None
    out_ref = refs.pop(0)
    if first:
        hh_ref, hl_ref = refs.pop(0), refs.pop(0)
        hh, hl = split(h_ref[...])
        hh_ref[...] = hh
        hl_ref[...] = hl
    _, _, _, c = place()
    cc = 1 - c if sibling else c
    if last:
        tmp, sem = refs
        low = pltpu.make_async_copy(low_ref, out_ref.at[pl.ds(0, 512), :], sem.at[0])
        low.start()
    rows = [x_ref[pl.ds(pl.multiple_of(512 * k + 256 * cc, 256), 256), :] for k in chunks]
    ah, al = split(jnp.concatenate(rows, axis=0))
    out = dot3(ah, al, hh_ref[...], hl_ref[...])
    if recv:
        out = out + recv_ref[...]
    if last:
        tmp[...] = out
        high = pltpu.make_async_copy(tmp, out_ref.at[pl.ds(512, 512), :], sem.at[1])
        high.start()
        low.wait()
        high.wait()
    else:
        out_ref[...] = out


def prod(spectra, h, chunks, sibling, recv=None, low=None):
    first = not isinstance(h, tuple)
    last = low is not None
    ins = [spectra] + ([h] if first else list(h)) + ([] if recv is None else [recv]) + ([low] if last else [])
    outs = [sds(1024 if last else 512, 512)]
    if first:
        outs += [sds(1024, 512, dtype=bf16)] * 2
    out = pl.pallas_call(
        functools.partial(prod_kernel, chunks, sibling, first, recv is not None, last),
        out_shape=outs,
        in_specs=[VM] * len(ins),
        out_specs=[HBM] if last else [VM] * len(outs),
        scratch_shapes=[pltpu.VMEM((512, 512), f32), pltpu.SemaphoreType.DMA((2,))] if last else [],
        compiler_params=params(14),
        cost_estimate=cost(6 * 512 * 1024 * 512, 6 << 20),
        name="prod",
    )(*ins)
    return out if first else out[0]


def flip_kernel(x_ref, th_ref, tl_ref):
    for k in range(0, 1024, 128):
        hi, lo = split(x_ref[:, k : k + 128].T)
        th_ref[0, k : k + 128, :] = hi
        tl_ref[0, k : k + 128, :] = lo


def flip(spectra):
    spec = pl.BlockSpec((1, 1024, 128), lambda i: (i, 0, 0))
    return pl.pallas_call(
        flip_kernel,
        grid=(16,),
        out_shape=[sds(16, 1024, 128, dtype=bf16)] * 2,
        in_specs=[pl.BlockSpec((128, 1024), lambda i: (i, 0))],
        out_specs=[spec, spec],
        compiler_params=params(6),
        cost_estimate=cost(1 << 24, 16 << 20),
        name="flip",
    )(spectra)


def back_kernel(chunks, later, last, *refs):
    refs = list(refs)
    th_ref, tl_ref = refs.pop(0), refs.pop(0)
    ws = [refs.pop(0) for _ in chunks]
    acc_ref = refs.pop(0) if later else None
    if later:
        refs.pop(0)
    outs, (w_out, sem) = refs[:-2], refs[-2:]
    z, y, x, c = place()
    at, copies = [], []
    for k, (r, sibling) in enumerate(chunks):
        first = 2 * (2 * ((x + r) % 4) + (1 - c if sibling else c))
        at += [first, first + 1]
        cp = pltpu.make_async_copy(ws[k], w_out.at[pl.ds(pl.multiple_of(128 * first, 256), 256), :], sem.at[k])
        cp.start()
        copies.append(cp)
    wh, wl = split(jnp.concatenate([w[...] for w in ws], axis=0))
    for half in range(2):
        if last:
            ring = y if half == 0 else z
            blocks = [pl.ds(pl.multiple_of(512 * half + 128 * ((ring + r) % 4), 128), 128) for r in REL]
        else:
            blocks = [pl.ds(512 * half, 512)]

        def left(ref):
            rows = [jnp.concatenate([ref[i, b, :] for i in at], axis=1) for b in blocks]
            return jnp.concatenate(rows, axis=0)

        out = dot3(left(th_ref), left(tl_ref), wh, wl)
        n = 512 // len(blocks)
        for k, b in enumerate(blocks):
            part = out[n * k : n * (k + 1)]
            if later:
                part = part + acc_ref[b, :]
            if last:
                outs[4 * half + k][...] = part
            else:
                outs[0][b, :] = part
    for cp in copies:
        cp.wait()


def back(flipped, ws, chunks, carry=(), last=False):
    ins = list(flipped) + list(ws) + list(carry)
    n = len(ins)
    outs = [sds(128, 512)] * 8 if last else [sds(1024, 512)]
    return pl.pallas_call(
        functools.partial(back_kernel, tuple(chunks), bool(carry), last),
        out_shape=outs + [sds(2048, 512)],
        in_specs=[VM] * (2 + len(ws)) + ([VM, HBM] if carry else []),
        out_specs=[VM] * len(outs) + [HBM],
        scratch_shapes=[pltpu.SemaphoreType.DMA((len(ws),))],
        input_output_aliases={n - 1: len(outs)} if carry else {},
        compiler_params=params(12),
        cost_estimate=cost(6 * 1024 * 512 * 256 * len(chunks), 6 << 20),
        name="back",
    )(*ins)


def gram_h_kernel(h_ref, _, mine_ref, theirs_ref, tmp):
    z, y, _, c = place()
    h = h_ref[...]
    tmp[...] = h.T
    left = tmp[pl.ds(pl.multiple_of(32 * (4 * z + y), 32), 32), :]
    both = dot3(*split(left), *split(h))
    first = (c == 0).astype(f32)
    mine_ref[...] = both[:16] * first + both[16:] * (1.0 - first)
    theirs_ref[...] = both[16:] * first + both[:16] * (1.0 - first)


def gram_h(h, hold):
    return pl.pallas_call(
        gram_h_kernel,
        out_shape=[sds(16, 512)] * 2,
        in_specs=[VM] * 2,
        out_specs=[VM] * 2,
        scratch_shapes=[pltpu.VMEM((512, 1024), f32)],
        compiler_params=params(14),
        cost_estimate=cost(6 * 512 * 32 * 1024, 4 << 20),
        name="gram_h",
    )(h, hold)


def gram_w_kernel(w_ref, ws_ref, *refs):
    outs, tmp = refs[:4], refs[4]
    _, _, x, c = place()
    right = jnp.concatenate([w_ref[...], ws_ref[...]], axis=0)
    tmp[...] = right.T
    rows = [tmp[pl.ds(pl.multiple_of(128 * ((x + r) % 4) + 64 * c, 64), 64), :] for r in REL]
    out = dot3(*split(jnp.concatenate(rows, axis=0)), *split(right))
    for k in range(4):
        outs[k][...] = out[64 * k : 64 * (k + 1)]


def gram_w(w, ws):
    return pl.pallas_call(
        gram_w_kernel,
        out_shape=[sds(64, 512)] * 4,
        in_specs=[VM] * 2,
        out_specs=[VM] * 4,
        scratch_shapes=[pltpu.VMEM((512, 512), f32)],
        compiler_params=params(10),
        cost_estimate=cost(6 * 256 * 512 * 512, 4 << 20),
        name="gram_w",
    )(w, ws)


def sweep_kernel(axis, nparts, *refs):
    parts, (start, mine, theirs), refs = refs[:nparts], refs[nparts : nparts + 3], refs[nparts + 3 :]
    outs, (g, gh, gl, fh, fl, ff, pp, sem) = refs[:-8], refs[-8:]
    z, y, x, c = place()
    n = ff.shape[0]
    if axis == "col":
        rows = [start]
    else:
        rows = [start.at[pl.ds(pl.multiple_of(row, 32), 32), :] for row in (128 * y + 32 * z, 512 + 128 * z + 32 * y)]
    n = n // len(rows)
    begin = [pltpu.make_async_copy(r, ff.at[pl.ds(n * k, n), :], sem.at[k]) for k, r in enumerate(rows)]
    for cp in begin:
        cp.start()
    for t, piece in enumerate((mine, theirs)):
        cc = c if t == 0 else 1 - c
        for j in range(4):
            if axis == "samp":
                row = 128 * ((x + REL[j]) % 4) + 64 * cc
                g[pl.ds(pl.multiple_of(row, 64), 64), :] = piece[64 * j : 64 * j + 64, :]
                continue
            for i in range(4):
                row = 32 * (4 * ((z + REL[i]) % 4) + (y + REL[j]) % 4) + 16 * cc
                g[pl.ds(pl.multiple_of(row, 16), 16), :] = piece[64 * j + 16 * i : 64 * j + 16 * i + 16, :]
    hi, lo = split(g[...])
    gh[...] = hi
    gl[...] = lo
    inv = []
    for b in range(0, 512, BLOCK):
        inv.append(1.0 / jnp.sum(g[b : b + BLOCK, b : b + BLOCK], axis=0, keepdims=True))
    pieces = [p[k : k + n, :] for p in parts for k in range(0, p.shape[0], n)]
    each = len(pieces) // len(rows)
    for k in range(len(rows)):
        total = pieces[each * k]
        for piece in pieces[each * k + 1 : each * (k + 1)]:
            total = total + piece
        pp[n * k : n * (k + 1), :] = total
    for cp in begin:
        cp.wait()
    hi, lo = split(ff[...])
    fh[...] = hi
    fl[...] = lo
    for _ in range(SWEEPS):
        for k, b in enumerate(range(0, 512, BLOCK)):
            cols = slice(b, b + BLOCK)
            fg = dot3(fh[...], fl[...], gh[:, cols], gl[:, cols])
            new = jnp.maximum(ff[:, cols] + (pp[:, cols] - fg) * inv[k], floor_value)
            ff[:, cols] = new
            hi, lo = split(new)
            fh[:, cols] = hi
            fl[:, cols] = lo
    for k, out in enumerate(outs):
        out[...] = ff[n * k : n * (k + 1), :]


def sweep(parts, start, axis, rows, pieces, nout):
    return pl.pallas_call(
        functools.partial(sweep_kernel, axis, len(parts)),
        out_shape=[sds(rows // nout, 512)] * nout,
        in_specs=[VM] * len(parts) + [VM if axis == "col" else HBM, VM, VM],
        out_specs=[VM] * nout,
        scratch_shapes=[
            pltpu.VMEM((512, 512), f32),
            pltpu.VMEM((512, 512), bf16),
            pltpu.VMEM((512, 512), bf16),
            pltpu.VMEM((rows, 512), bf16),
            pltpu.VMEM((rows, 512), bf16),
            pltpu.VMEM((rows, 512), f32),
            pltpu.VMEM((rows, 512), f32),
            pltpu.SemaphoreType.DMA((2,)),
        ],
        compiler_params=params(12 if axis == "col" else 30),
        cost_estimate=cost(72 * rows * 512 * 512, 4 << 20),
        name="sweep",
    )(*parts, start, *pieces)


def take_kernel(w_ref, out_ref, sem):
    _, _, x, c = place()
    rows = w_ref.at[pl.ds(pl.multiple_of(256 * (2 * x + c), 256), 256), :]
    cp = pltpu.make_async_copy(rows, out_ref, sem)
    cp.start()
    cp.wait()


def take(w_start):
    return pl.pallas_call(
        take_kernel,
        out_shape=sds(256, 512),
        in_specs=[HBM],
        out_specs=VM,
        scratch_shapes=[pltpu.SemaphoreType.DMA],
        compiler_params=params(57),
        cost_estimate=cost(0, 1 << 20),
        name="take",
    )(w_start)


def lay_h_kernel(*refs):
    ins, out = refs[:8], refs[8]
    z, y, _, _ = place()
    for half in range(2):
        big, small = (y, z) if half == 0 else (z, y)
        for j in range(4):
            for i in range(4):
                row = pl.multiple_of(512 * half + 128 * ((big + REL[j]) % 4) + 32 * ((small + REL[i]) % 4), 32)
                out[pl.ds(row, 32), :] = ins[4 * half + j][32 * i : 32 * (i + 1), :]


def lay_h(pieces):
    return pl.pallas_call(
        lay_h_kernel,
        out_shape=sds(1024, 512),
        in_specs=[VM] * 8,
        out_specs=VM,
        compiler_params=params(6),
        cost_estimate=cost(0, 4 << 20),
        name="lay_h",
    )(*pieces)


def halve_kernel(*refs):
    z, y, _, _ = place()
    tmp = refs[16]
    for half in range(2):
        a, b, c, d = refs[4 * half : 4 * half + 4]
        tmp[...] = (a[...] + b[...]) + (c[...] + d[...])
        ring = z if half == 0 else y
        for k in range(4):
            refs[8 + 4 * half + k][...] = tmp[pl.ds(pl.multiple_of(32 * ((ring + REL[k]) % 4), 32), 32), :]


def halve(parts):
    return pl.pallas_call(
        halve_kernel,
        out_shape=[sds(32, 512)] * 8,
        in_specs=[VM] * 8,
        out_specs=[VM] * 8,
        scratch_shapes=[pltpu.VMEM((128, 512), f32)],
        compiler_params=params(6),
        cost_estimate=cost(1 << 19, 3 << 20),
        name="halve",
    )(*parts)


def moves(axis, dim):
    out = {}
    for r in range(4):
        pairs = []
        if axis == "col":
            for i in range(8):
                x, c = i // 2, i % 2
                pairs.append((i, 2 * x + 1 - c) if dim == "core" else (i, 2 * ((x + r) % 4) + c))
        else:
            for i in range(16):
                z, y = i // 4, i % 4
                pairs.append((i, 4 * ((z + r) % 4) + y) if dim == "z" else (i, 4 * z + (y + r) % 4))
        out[r] = pairs
    return out


XGROUPS = [[0, 2, 4, 6], [1, 3, 5, 7]]
CORE, X = moves("col", "core"), moves("col", "x")
Y, Z = moves("samp", "y"), moves("samp", "z")


def swap(a):
    return lax.ppermute(a, "col", CORE[0])


def send(a, axis, table, r):
    return lax.ppermute(a, axis, table[r])


def fetch(a, axis, table):
    return [lax.ppermute(a, axis, table[(4 - r) % 4]) for r in REL[1:]]


def after(a, *others):
    return lax.optimization_barrier((a,) + others)[0]


def join_kernel(nout, *refs):
    ins, outs = refs[:-nout], refs[-nout:]
    n = len(ins) // nout
    for k, out in enumerate(outs):
        rows = ins[n * k].shape[0]
        for i in range(n):
            out[rows * i : rows * (i + 1), :] = ins[n * k + i][...]


def join(parts, nout=1):
    rows = parts[0].shape[0] * len(parts) // nout
    out = pl.pallas_call(
        functools.partial(join_kernel, nout),
        out_shape=[sds(rows, 512)] * nout,
        in_specs=[VM] * len(parts),
        out_specs=[VM] * nout,
        compiler_params=params(4),
        cost_estimate=cost(0, rows * nout * 4096),
        name="join",
    )(*parts)
    return out if nout > 1 else out[0]


def add_kernel(n, *refs):
    total = refs[0][...]
    for r in refs[1:n]:
        total = total + r[...]
    refs[-1][...] = total


def add(parts):
    rows = parts[0].shape[0]
    return pl.pallas_call(
        functools.partial(add_kernel, len(parts)),
        out_shape=sds(rows, 512),
        in_specs=[VM] * len(parts),
        out_specs=VM,
        compiler_params=params(4),
        cost_estimate=cost(rows * 512 * len(parts), rows * 4096 * len(parts)),
        name="add",
    )(*parts)


def deal(pieces, axis, table):
    return [pieces[0]] + [send(pieces[k], axis, table, REL[k]) for k in (1, 2, 3)]


def spread(strip):
    strip = join([strip] + fetch(strip, "samp", Z))
    return join([strip] + fetch(strip, "samp", Y))


def shards(spectra, w_start, h_start):
    g_mine, g_theirs = gram_h(h_start, spectra)
    strip = add([g_mine, swap(g_theirs)])

    a1, hh, hl = prod(spectra, after(h_start, strip), (0, 1), True)
    r1 = swap(a1)
    strip = add([after(strip, a1)] + fetch(strip, "col", X))
    h = (after(hh, strip), hl)
    a2 = prod(spectra, h, (2, 3), True)
    r2 = swap(a2)
    low = prod(spectra, h, (0, 1), False, after(r1, a2))
    both = prod(spectra, h, (2, 3), False, r2, low)
    product = lax.all_to_all(both, "col", 0, 0, axis_index_groups=XGROUPS, tiled=True)

    part = spread(after(strip, both))
    w0 = take(after(w_start, part))
    (w,) = sweep([product], w0, "col", 256, (part, swap(part)), 1)

    ws = swap(w)
    slices = gram_w(w, ws)
    flipped = flip(after(spectra, slices[0]))
    slices = deal(slices, "col", X)
    part = add([after(slices[0], *flipped)] + slices[1:])
    late = after(w, part)
    near_p, near_m, far = send(late, "col", X, 3), send(late, "col", X, 1), send(late, "col", X, 2)
    carry = back(flipped, (w, after(ws, part)), ((0, False), (0, True)))
    part = add([after(part, carry[0])] + fetch(part, "samp", Y))
    near_p, near_m = after(near_p, part), after(near_m, part)
    sib_p, sib_m = swap(near_p), swap(near_m)
    carry = back(flipped, (near_p, near_m), ((1, False), (3, False)), carry)
    part = add([after(part, carry[0])] + fetch(part, "samp", Z))
    carry = back(flipped, (sib_p, sib_m), ((1, True), (3, True)), carry)
    sib_f = swap(after(far, part))
    part = join([after(part, carry[0])] + fetch(part, "col", X))
    carry = (after(carry[0], part), carry[1])
    *out, w_out = back(flipped, (far, sib_f), ((2, False), (2, True)), carry, True)

    parts = halve(deal(out[:4], "samp", Y) + deal(out[4:], "samp", Z))
    part = after(part, out[0])
    parts = deal(parts[:4], "samp", Z) + deal(parts[4:], "samp", Y)
    ha, hb = sweep(parts, h_start, "samp", 64, (part, swap(part)), 2)

    row_a, row_b = join([ha] + fetch(ha, "samp", Z) + [hb] + fetch(hb, "samp", Y), 2)
    h_out = lay_h([row_a] + fetch(row_a, "samp", Y) + [row_b] + fetch(row_b, "samp", Z))
    return (w_out, h_out)


def solution(mesh):
    return jax.shard_map(
        shards,
        mesh=mesh,
        in_specs=(P("samp", "col"), P("samp", None), P("col", None)),
        out_specs=(P("samp", None), P("col", None)),
        check_vma=False,
    )
```

```python
import functools
import jax
import jax.numpy as jnp
from jax import lax
from jax.experimental import pallas as pl
from jax.experimental.pallas import tpu as pltpu
from jax.sharding import PartitionSpec as P

BLOCK = 128
SWEEPS = 3
floor_value = 1e-06
REL = (0, 1, 3, 2)
f32, bf16 = jnp.float32, jnp.bfloat16
ANY = pl.BlockSpec(memory_space=pl.ANY)
HBM = pl.BlockSpec(memory_space=pltpu.HBM)
VM = pl.BlockSpec(memory_space=pltpu.VMEM)


def sds(*shape, dtype=f32):
    return jax.ShapeDtypeStruct(shape, dtype)


def cost(flops, nbytes):
    return pl.CostEstimate(flops=flops, bytes_accessed=nbytes, transcendentals=0)


def params(mib):
    return pltpu.CompilerParams(vmem_limit_bytes=mib << 20)


def split(a):
    hi = a.astype(bf16)
    return hi, (a - hi.astype(f32)).astype(bf16)


def dot3(ah, al, bh, bl):
    d = functools.partial(jnp.dot, preferred_element_type=f32)
    return d(ah, bh) + (d(ah, bl) + d(al, bh))


def place():
    s, q = lax.axis_index("samp"), lax.axis_index("col")
    return s // 4, s % 4, q // 2, q % 2


def prod_kernel(chunks, sibling, first, recv, last, *refs):
    refs = list(refs)
    x_ref = refs.pop(0)
    if first:
        h_ref = refs.pop(0)
    else:
        hh_ref, hl_ref = refs.pop(0), refs.pop(0)
    recv_ref = refs.pop(0) if recv else None
    low_ref = refs.pop(0) if last else None
    out_ref = refs.pop(0)
    if first:
        hh_ref, hl_ref = refs.pop(0), refs.pop(0)
        hh, hl = split(h_ref[...])
        hh_ref[...] = hh
        hl_ref[...] = hl
    _, _, _, c = place()
    cc = 1 - c if sibling else c
    if last:
        tmp, sem = refs
        low = pltpu.make_async_copy(low_ref, out_ref.at[pl.ds(0, 512), :], sem.at[0])
        low.start()
    rows = [x_ref[pl.ds(pl.multiple_of(512 * k + 256 * cc, 256), 256), :] for k in chunks]
    ah, al = split(jnp.concatenate(rows, axis=0))
    out = dot3(ah, al, hh_ref[...], hl_ref[...])
    if recv:
        out = out + recv_ref[...]
    if last:
        tmp[...] = out
        high = pltpu.make_async_copy(tmp, out_ref.at[pl.ds(512, 512), :], sem.at[1])
        high.start()
        low.wait()
        high.wait()
    else:
        out_ref[...] = out


def prod(spectra, h, chunks, sibling, recv=None, low=None):
    first = not isinstance(h, tuple)
    last = low is not None
    ins = [spectra] + ([h] if first else list(h)) + ([] if recv is None else [recv]) + ([low] if last else [])
    outs = [sds(1024 if last else 512, 512)]
    if first:
        outs += [sds(1024, 512, dtype=bf16)] * 2
    out = pl.pallas_call(
        functools.partial(prod_kernel, chunks, sibling, first, recv is not None, last),
        out_shape=outs,
        in_specs=[VM] * len(ins),
        out_specs=[HBM] if last else [VM] * len(outs),
        scratch_shapes=[pltpu.VMEM((512, 512), f32), pltpu.SemaphoreType.DMA((2,))] if last else [],
        compiler_params=params(14),
        cost_estimate=cost(6 * 512 * 1024 * 512, 6 << 20),
        name="prod",
    )(*ins)
    return out if first else out[0]


def flip_kernel(x_ref, th_ref, tl_ref):
    for k in range(0, 1024, 128):
        hi, lo = split(x_ref[:, k : k + 128].T)
        th_ref[0, k : k + 128, :] = hi
        tl_ref[0, k : k + 128, :] = lo


def flip(spectra):
    spec = pl.BlockSpec((1, 1024, 128), lambda i: (i, 0, 0))
    return pl.pallas_call(
        flip_kernel,
        grid=(16,),
        out_shape=[sds(16, 1024, 128, dtype=bf16)] * 2,
        in_specs=[pl.BlockSpec((128, 1024), lambda i: (i, 0))],
        out_specs=[spec, spec],
        compiler_params=params(6),
        cost_estimate=cost(1 << 24, 16 << 20),
        name="flip",
    )(spectra)


def back_kernel(chunks, later, *refs):
    refs = list(refs)
    th_ref, tl_ref = refs.pop(0), refs.pop(0)
    ws = [refs.pop(0) for _ in chunks]
    acc_ref = refs.pop(0) if later else None
    if later:
        refs.pop(0)
    out_ref, w_out, sem = refs[:3]
    z, y, x, c = place()
    at, copies = [], []
    for k, (r, sibling) in enumerate(chunks):
        first = 2 * (2 * ((x + r) % 4) + (1 - c if sibling else c))
        at += [first, first + 1]
        cp = pltpu.make_async_copy(ws[k], w_out.at[pl.ds(pl.multiple_of(128 * first, 256), 256), :], sem.at[k])
        cp.start()
        copies.append(cp)
    wh, wl = split(jnp.concatenate([w[...] for w in ws], axis=0))
    for k in range(0, 1024, 512):
        rows = slice(k, k + 512)
        ah = jnp.concatenate([th_ref[i, rows, :] for i in at], axis=1)
        al = jnp.concatenate([tl_ref[i, rows, :] for i in at], axis=1)
        out = dot3(ah, al, wh, wl)
        if later:
            out = out + acc_ref[rows, :]
        if len(refs) > 3:
            refs[3][rows, :] = out
            cp = pltpu.make_async_copy(refs[3].at[rows, :], out_ref.at[rows, :], sem.at[2 + k // 512])
            cp.start()
            copies.append(cp)
        else:
            out_ref[rows, :] = out
    for cp in copies:
        cp.wait()


def back(flipped, ws, chunks, carry=(), last=False):
    ins = list(flipped) + list(ws) + list(carry)
    n = len(ins)
    return pl.pallas_call(
        functools.partial(back_kernel, tuple(chunks), bool(carry)),
        out_shape=[sds(1024, 512), sds(2048, 512)],
        in_specs=[VM] * (2 + len(ws)) + ([VM, HBM] if carry else []),
        out_specs=[HBM if last else VM, HBM],
        scratch_shapes=[pltpu.SemaphoreType.DMA((4,))] + ([pltpu.VMEM((1024, 512), f32)] if last else []),
        input_output_aliases={n - 1: 1} if carry else {},
        compiler_params=params(12),
        cost_estimate=cost(6 * 1024 * 512 * 256 * len(chunks), 6 << 20),
        name="back",
    )(*ins)


def gram_h_kernel(h_ref, _, mine_ref, theirs_ref, tmp):
    z, y, _, c = place()
    h = h_ref[...]
    tmp[...] = h.T
    left = tmp[pl.ds(pl.multiple_of(32 * (4 * z + y), 32), 32), :]
    both = dot3(*split(left), *split(h))
    first = (c == 0).astype(f32)
    mine_ref[...] = both[:16] * first + both[16:] * (1.0 - first)
    theirs_ref[...] = both[16:] * first + both[:16] * (1.0 - first)


def gram_h(h, hold):
    return pl.pallas_call(
        gram_h_kernel,
        out_shape=[sds(16, 512)] * 2,
        in_specs=[VM] * 2,
        out_specs=[VM] * 2,
        scratch_shapes=[pltpu.VMEM((512, 1024), f32)],
        compiler_params=params(14),
        cost_estimate=cost(6 * 512 * 32 * 1024, 4 << 20),
        name="gram_h",
    )(h, hold)


def gram_w_kernel(w_ref, ws_ref, *refs):
    outs, tmp = refs[:4], refs[4]
    _, _, x, c = place()
    right = jnp.concatenate([w_ref[...], ws_ref[...]], axis=0)
    tmp[...] = right.T
    rows = [tmp[pl.ds(pl.multiple_of(128 * ((x + r) % 4) + 64 * c, 64), 64), :] for r in REL]
    out = dot3(*split(jnp.concatenate(rows, axis=0)), *split(right))
    for k in range(4):
        outs[k][...] = out[64 * k : 64 * (k + 1)]


def gram_w(w, ws):
    return pl.pallas_call(
        gram_w_kernel,
        out_shape=[sds(64, 512)] * 4,
        in_specs=[VM] * 2,
        out_specs=[VM] * 4,
        scratch_shapes=[pltpu.VMEM((512, 512), f32)],
        compiler_params=params(10),
        cost_estimate=cost(6 * 256 * 512 * 512, 4 << 20),
        name="gram_w",
    )(w, ws)


def sweep_kernel(axis, product, start, mine, theirs, *refs):
    outs, (g, gh, gl, fh, fl, ff, pp, sem) = refs[:-8], refs[-8:]
    z, y, x, c = place()
    n = ff.shape[0]
    if axis == "col":
        rows = start
    else:
        rows = start.at[pl.ds(pl.multiple_of(n * (4 * z + y), n), n), :]
    begin = pltpu.make_async_copy(rows, ff, sem)
    begin.start()
    for t, piece in enumerate((mine, theirs)):
        cc = c if t == 0 else 1 - c
        for j in range(4):
            if axis == "samp":
                row = 128 * ((x + REL[j]) % 4) + 64 * cc
                g[pl.ds(pl.multiple_of(row, 64), 64), :] = piece[64 * j : 64 * j + 64, :]
                continue
            for i in range(4):
                row = 32 * (4 * ((z + REL[i]) % 4) + (y + REL[j]) % 4) + 16 * cc
                g[pl.ds(pl.multiple_of(row, 16), 16), :] = piece[64 * j + 16 * i : 64 * j + 16 * i + 16, :]
    hi, lo = split(g[...])
    gh[...] = hi
    gl[...] = lo
    inv = []
    for b in range(0, 512, BLOCK):
        inv.append(1.0 / jnp.sum(g[b : b + BLOCK, b : b + BLOCK], axis=0, keepdims=True))
    total = product[:n, :]
    for k in range(n, product.shape[0], n):
        total = total + product[k : k + n, :]
    pp[...] = total
    begin.wait()
    hi, lo = split(ff[...])
    fh[...] = hi
    fl[...] = lo
    for _ in range(SWEEPS):
        for k, b in enumerate(range(0, 512, BLOCK)):
            cols = slice(b, b + BLOCK)
            fg = dot3(fh[...], fl[...], gh[:, cols], gl[:, cols])
            new = jnp.maximum(ff[:, cols] + (pp[:, cols] - fg) * inv[k], floor_value)
            ff[:, cols] = new
            hi, lo = split(new)
            fh[:, cols] = hi
            fl[:, cols] = lo
    n = n // len(outs)
    for k, out in enumerate(outs):
        out[...] = ff[n * k : n * (k + 1), :]


def sweep(product, start, axis, rows, pieces, nout):
    return pl.pallas_call(
        functools.partial(sweep_kernel, axis),
        out_shape=[sds(rows // nout, 512)] * nout,
        in_specs=[VM, VM if axis == "col" else HBM, VM, VM],
        out_specs=[VM] * nout,
        scratch_shapes=[
            pltpu.VMEM((512, 512), f32),
            pltpu.VMEM((512, 512), bf16),
            pltpu.VMEM((512, 512), bf16),
            pltpu.VMEM((rows, 512), bf16),
            pltpu.VMEM((rows, 512), bf16),
            pltpu.VMEM((rows, 512), f32),
            pltpu.VMEM((rows, 512), f32),
            pltpu.SemaphoreType.DMA,
        ],
        compiler_params=params(12 if axis == "col" else 50),
        cost_estimate=cost(72 * rows * 512 * 512, 4 << 20),
        name="sweep",
    )(product, start, *pieces)


def take_kernel(w_ref, out_ref, sem):
    _, _, x, c = place()
    rows = w_ref.at[pl.ds(pl.multiple_of(256 * (2 * x + c), 256), 256), :]
    cp = pltpu.make_async_copy(rows, out_ref, sem)
    cp.start()
    cp.wait()


def take(w_start):
    return pl.pallas_call(
        take_kernel,
        out_shape=sds(256, 512),
        in_specs=[HBM],
        out_specs=VM,
        scratch_shapes=[pltpu.SemaphoreType.DMA],
        compiler_params=params(57),
        cost_estimate=cost(0, 1 << 20),
        name="take",
    )(w_start)


def lay_h_kernel(*refs):
    ins, out = refs[:8], refs[8]
    z, y, _, _ = place()
    for half in range(2):
        for j in range(4):
            for i in range(4):
                dz, dy = (REL[i], REL[j]) if half == 0 else (REL[j], REL[i])
                row = pl.multiple_of(64 * (4 * ((z + dz) % 4) + (y + dy) % 4) + 32 * half, 32)
                out[pl.ds(row, 32), :] = ins[4 * half + j][32 * i : 32 * (i + 1), :]


def lay_h(pieces):
    return pl.pallas_call(
        lay_h_kernel,
        out_shape=sds(1024, 512),
        in_specs=[VM] * 8,
        out_specs=VM,
        compiler_params=params(6),
        cost_estimate=cost(0, 4 << 20),
        name="lay_h",
    )(*pieces)


def moves(axis, dim):
    out = {}
    for r in range(4):
        pairs = []
        if axis == "col":
            for i in range(8):
                x, c = i // 2, i % 2
                pairs.append((i, 2 * x + 1 - c) if dim == "core" else (i, 2 * ((x + r) % 4) + c))
        else:
            for i in range(16):
                z, y = i // 4, i % 4
                pairs.append((i, 4 * ((z + r) % 4) + y) if dim == "z" else (i, 4 * z + (y + r) % 4))
        out[r] = pairs
    return out


XGROUPS = [[0, 2, 4, 6], [1, 3, 5, 7]]
CORE, X = moves("col", "core"), moves("col", "x")
Y, Z = moves("samp", "y"), moves("samp", "z")


def swap(a):
    return lax.ppermute(a, "col", CORE[0])


def send(a, axis, table, r):
    return lax.ppermute(a, axis, table[r])


def fetch(a, axis, table):
    return [lax.ppermute(a, axis, table[(4 - r) % 4]) for r in REL[1:]]


def after(a, *others):
    return lax.optimization_barrier((a,) + others)[0]


def join_kernel(nout, *refs):
    ins, outs = refs[:-nout], refs[-nout:]
    n = len(ins) // nout
    for k, out in enumerate(outs):
        rows = ins[n * k].shape[0]
        for i in range(n):
            out[rows * i : rows * (i + 1), :] = ins[n * k + i][...]


def join(parts, nout=1):
    rows = parts[0].shape[0] * len(parts) // nout
    out = pl.pallas_call(
        functools.partial(join_kernel, nout),
        out_shape=[sds(rows, 512)] * nout,
        in_specs=[VM] * len(parts),
        out_specs=[VM] * nout,
        compiler_params=params(4),
        cost_estimate=cost(0, rows * nout * 4096),
        name="join",
    )(*parts)
    return out if nout > 1 else out[0]


def add_kernel(n, *refs):
    total = refs[0][...]
    for r in refs[1:n]:
        total = total + r[...]
    refs[-1][...] = total


def add(parts):
    rows = parts[0].shape[0]
    return pl.pallas_call(
        functools.partial(add_kernel, len(parts)),
        out_shape=sds(rows, 512),
        in_specs=[VM] * len(parts),
        out_specs=VM,
        compiler_params=params(4),
        cost_estimate=cost(rows * 512 * len(parts), rows * 4096 * len(parts)),
        name="add",
    )(*parts)


def deal(pieces, axis, table):
    return [pieces[0]] + [send(pieces[k], axis, table, REL[k]) for k in (1, 2, 3)]


def spread(strip):
    strip = join([strip] + fetch(strip, "samp", Z))
    return join([strip] + fetch(strip, "samp", Y))


def shards(spectra, w_start, h_start):
    g_mine, g_theirs = gram_h(h_start, spectra)
    strip = add([g_mine, swap(g_theirs)])

    a1, hh, hl = prod(spectra, after(h_start, strip), (0, 1), True)
    r1 = swap(a1)
    strip = add([after(strip, a1)] + fetch(strip, "col", X))
    h = (after(hh, strip), hl)
    a2 = prod(spectra, h, (2, 3), True)
    r2 = swap(a2)
    low = prod(spectra, h, (0, 1), False, after(r1, a2))
    both = prod(spectra, h, (2, 3), False, r2, low)
    product = lax.all_to_all(both, "col", 0, 0, axis_index_groups=XGROUPS, tiled=True)

    part = spread(after(strip, both))
    w0 = take(after(w_start, part))
    (w,) = sweep(product, w0, "col", 256, (part, swap(part)), 1)

    ws = swap(w)
    slices = gram_w(w, ws)
    flipped = flip(after(spectra, slices[0]))
    slices = deal(slices, "col", X)
    part = add([after(slices[0], *flipped)] + slices[1:])
    late = after(w, *flipped)
    near_p, near_m, far = send(late, "col", X, 3), send(late, "col", X, 1), send(late, "col", X, 2)
    carry = back(flipped, (w, after(ws, part)), ((0, False), (0, True)))
    part = add([after(part, carry[0])] + fetch(part, "samp", Y))
    near_p, near_m = after(near_p, part), after(near_m, part)
    sib_p, sib_m = swap(near_p), swap(near_m)
    carry = back(flipped, (near_p, near_m), ((1, False), (3, False)), carry)
    part = add([after(part, carry[0])] + fetch(part, "samp", Z))
    carry = back(flipped, (sib_p, sib_m), ((1, True), (3, True)), carry)
    sib_f = swap(after(far, part))
    carry = (after(carry[0], part), carry[1])
    back_sum, w_out = back(flipped, (far, sib_f), ((2, False), (2, True)), carry, True)

    product = lax.all_to_all(back_sum, "samp", 0, 0, tiled=True)
    part = after(part, back_sum)
    part = join([part] + fetch(part, "col", X))
    ha, hb = sweep(product, h_start, "samp", 64, (part, swap(part)), 2)

    row_a, row_b = join([ha] + fetch(ha, "samp", Z) + [hb] + fetch(hb, "samp", Y), 2)
    h_out = lay_h([row_a] + fetch(row_a, "samp", Y) + [row_b] + fetch(row_b, "samp", Z))
    return (w_out, h_out)


def solution(mesh):
    return jax.shard_map(
        shards,
        mesh=mesh,
        in_specs=(P("samp", "col"), P("samp", None), P("col", None)),
        out_specs=(P("samp", None), P("col", None)),
        check_vma=False,
    )
```

```python
import functools
import jax
import jax.numpy as jnp
from jax import lax
from jax.experimental import pallas as pl
from jax.experimental.pallas import tpu as pltpu
from jax.sharding import PartitionSpec as P

BLOCK = 128
SWEEPS = 3
floor_value = 1e-06
REL = (0, 1, 3, 2)
f32, bf16 = jnp.float32, jnp.bfloat16
ANY = pl.BlockSpec(memory_space=pl.ANY)
HBM = pl.BlockSpec(memory_space=pltpu.HBM)
VM = pl.BlockSpec(memory_space=pltpu.VMEM)


def sds(*shape, dtype=f32):
    return jax.ShapeDtypeStruct(shape, dtype)


def cost(flops, nbytes):
    return pl.CostEstimate(flops=flops, bytes_accessed=nbytes, transcendentals=0)


def params(mib):
    return pltpu.CompilerParams(vmem_limit_bytes=mib << 20)


def split(a):
    hi = a.astype(bf16)
    return hi, (a - hi.astype(f32)).astype(bf16)


def dot3(ah, al, bh, bl):
    d = functools.partial(jnp.dot, preferred_element_type=f32)
    return d(ah, bh) + (d(ah, bl) + d(al, bh))


def place():
    s, q = lax.axis_index("samp"), lax.axis_index("col")
    return s // 4, s % 4, q // 2, q % 2


def prod_kernel(chunks, sibling, first, recv, last, *refs):
    refs = list(refs)
    x_ref = refs.pop(0)
    if first:
        h_ref = refs.pop(0)
    else:
        hh_ref, hl_ref = refs.pop(0), refs.pop(0)
    recv_ref = refs.pop(0) if recv else None
    low_ref = refs.pop(0) if last else None
    out_ref = refs.pop(0)
    if first:
        hh_ref, hl_ref = refs.pop(0), refs.pop(0)
        hh, hl = split(h_ref[...])
        hh_ref[...] = hh
        hl_ref[...] = hl
    _, _, _, c = place()
    cc = 1 - c if sibling else c
    if last:
        tmp, sem = refs
        low = pltpu.make_async_copy(low_ref, out_ref.at[pl.ds(0, 512), :], sem.at[0])
        low.start()
    rows = [x_ref[pl.ds(pl.multiple_of(512 * k + 256 * cc, 256), 256), :] for k in chunks]
    ah, al = split(jnp.concatenate(rows, axis=0))
    out = dot3(ah, al, hh_ref[...], hl_ref[...])
    if recv:
        out = out + recv_ref[...]
    if last:
        tmp[...] = out
        high = pltpu.make_async_copy(tmp, out_ref.at[pl.ds(512, 512), :], sem.at[1])
        high.start()
        low.wait()
        high.wait()
    else:
        out_ref[...] = out


def prod(spectra, h, chunks, sibling, recv=None, low=None):
    first = not isinstance(h, tuple)
    last = low is not None
    ins = [spectra] + ([h] if first else list(h)) + ([] if recv is None else [recv]) + ([low] if last else [])
    outs = [sds(1024 if last else 512, 512)]
    if first:
        outs += [sds(1024, 512, dtype=bf16)] * 2
    out = pl.pallas_call(
        functools.partial(prod_kernel, chunks, sibling, first, recv is not None, last),
        out_shape=outs,
        in_specs=[VM] * len(ins),
        out_specs=[HBM] if last else [VM] * len(outs),
        scratch_shapes=[pltpu.VMEM((512, 512), f32), pltpu.SemaphoreType.DMA((2,))] if last else [],
        compiler_params=params(14),
        cost_estimate=cost(6 * 512 * 1024 * 512, 6 << 20),
        name="prod",
    )(*ins)
    return out if first else out[0]


def flip_kernel(x_ref, th_ref, tl_ref):
    for k in range(0, 1024, 128):
        hi, lo = split(x_ref[:, k : k + 128].T)
        th_ref[0, k : k + 128, :] = hi
        tl_ref[0, k : k + 128, :] = lo


def flip(spectra):
    spec = pl.BlockSpec((1, 1024, 128), lambda i: (i, 0, 0))
    return pl.pallas_call(
        flip_kernel,
        grid=(16,),
        out_shape=[sds(16, 1024, 128, dtype=bf16)] * 2,
        in_specs=[pl.BlockSpec((128, 1024), lambda i: (i, 0))],
        out_specs=[spec, spec],
        compiler_params=params(6),
        cost_estimate=cost(1 << 24, 16 << 20),
        name="flip",
    )(spectra)


def back_kernel(chunks, later, *refs):
    refs = list(refs)
    th_ref, tl_ref = refs.pop(0), refs.pop(0)
    ws = [refs.pop(0) for _ in chunks]
    acc_ref = refs.pop(0) if later else None
    if later:
        refs.pop(0)
    out_ref, w_out, sem = refs[:3]
    z, y, x, c = place()
    at, copies = [], []
    for k, (r, sibling) in enumerate(chunks):
        first = 2 * (2 * ((x + r) % 4) + (1 - c if sibling else c))
        at += [first, first + 1]
        cp = pltpu.make_async_copy(ws[k], w_out.at[pl.ds(pl.multiple_of(128 * first, 256), 256), :], sem.at[k])
        cp.start()
        copies.append(cp)
    wh, wl = split(jnp.concatenate([w[...] for w in ws], axis=0))
    for k in range(0, 1024, 512):
        rows = slice(k, k + 512)
        ah = jnp.concatenate([th_ref[i, rows, :] for i in at], axis=1)
        al = jnp.concatenate([tl_ref[i, rows, :] for i in at], axis=1)
        out = dot3(ah, al, wh, wl)
        if later:
            out = out + acc_ref[rows, :]
        if len(refs) > 3:
            refs[3][rows, :] = out
            cp = pltpu.make_async_copy(refs[3].at[rows, :], out_ref.at[rows, :], sem.at[2 + k // 512])
            cp.start()
            copies.append(cp)
        else:
            out_ref[rows, :] = out
    for cp in copies:
        cp.wait()


def back(flipped, ws, chunks, carry=(), last=False):
    ins = list(flipped) + list(ws) + list(carry)
    n = len(ins)
    return pl.pallas_call(
        functools.partial(back_kernel, tuple(chunks), bool(carry)),
        out_shape=[sds(1024, 512), sds(2048, 512)],
        in_specs=[VM] * (2 + len(ws)) + ([VM, HBM] if carry else []),
        out_specs=[HBM if last else VM, HBM],
        scratch_shapes=[pltpu.SemaphoreType.DMA((4,))] + ([pltpu.VMEM((1024, 512), f32)] if last else []),
        input_output_aliases={n - 1: 1} if carry else {},
        compiler_params=params(12),
        cost_estimate=cost(6 * 1024 * 512 * 256 * len(chunks), 6 << 20),
        name="back",
    )(*ins)


def gram_h_kernel(h_ref, _, mine_ref, theirs_ref, tmp):
    z, y, _, c = place()
    h = h_ref[...]
    tmp[...] = h.T
    left = tmp[pl.ds(pl.multiple_of(32 * (4 * z + y), 32), 32), :]
    both = dot3(*split(left), *split(h))
    first = (c == 0).astype(f32)
    mine_ref[...] = both[:16] * first + both[16:] * (1.0 - first)
    theirs_ref[...] = both[16:] * first + both[:16] * (1.0 - first)


def gram_h(h, hold):
    return pl.pallas_call(
        gram_h_kernel,
        out_shape=[sds(16, 512)] * 2,
        in_specs=[VM] * 2,
        out_specs=[VM] * 2,
        scratch_shapes=[pltpu.VMEM((512, 1024), f32)],
        compiler_params=params(14),
        cost_estimate=cost(6 * 512 * 32 * 1024, 4 << 20),
        name="gram_h",
    )(h, hold)


def gram_w_kernel(w_ref, ws_ref, *refs):
    outs, tmp = refs[:4], refs[4]
    _, _, x, c = place()
    right = jnp.concatenate([w_ref[...], ws_ref[...]], axis=0)
    tmp[...] = right.T
    rows = [tmp[pl.ds(pl.multiple_of(128 * ((x + r) % 4) + 64 * c, 64), 64), :] for r in REL]
    out = dot3(*split(jnp.concatenate(rows, axis=0)), *split(right))
    for k in range(4):
        outs[k][...] = out[64 * k : 64 * (k + 1)]


def gram_w(w, ws):
    return pl.pallas_call(
        gram_w_kernel,
        out_shape=[sds(64, 512)] * 4,
        in_specs=[VM] * 2,
        out_specs=[VM] * 4,
        scratch_shapes=[pltpu.VMEM((512, 512), f32)],
        compiler_params=params(10),
        cost_estimate=cost(6 * 256 * 512 * 512, 4 << 20),
        name="gram_w",
    )(w, ws)


def sweep_kernel(axis, product, start, mine, theirs, *refs):
    outs, (g, gh, gl, fh, fl, ff, pp, sem) = refs[:-8], refs[-8:]
    z, y, x, c = place()
    n = ff.shape[0]
    first = n * (2 * x + c if axis == "col" else 4 * z + y)
    rows = start.at[pl.ds(pl.multiple_of(first, n), n), :]
    begin = pltpu.make_async_copy(rows, ff, sem)
    begin.start()
    for t, piece in enumerate((mine, theirs)):
        cc = c if t == 0 else 1 - c
        for j in range(4):
            if axis == "samp":
                row = 128 * ((x + REL[j]) % 4) + 64 * cc
                g[pl.ds(pl.multiple_of(row, 64), 64), :] = piece[64 * j : 64 * j + 64, :]
                continue
            for i in range(4):
                row = 32 * (4 * ((z + REL[i]) % 4) + (y + REL[j]) % 4) + 16 * cc
                g[pl.ds(pl.multiple_of(row, 16), 16), :] = piece[64 * j + 16 * i : 64 * j + 16 * i + 16, :]
    hi, lo = split(g[...])
    gh[...] = hi
    gl[...] = lo
    inv = []
    for b in range(0, 512, BLOCK):
        inv.append(1.0 / jnp.sum(g[b : b + BLOCK, b : b + BLOCK], axis=0, keepdims=True))
    total = product[:n, :]
    for k in range(n, product.shape[0], n):
        total = total + product[k : k + n, :]
    pp[...] = total
    begin.wait()
    hi, lo = split(ff[...])
    fh[...] = hi
    fl[...] = lo
    for _ in range(SWEEPS):
        for k, b in enumerate(range(0, 512, BLOCK)):
            cols = slice(b, b + BLOCK)
            fg = dot3(fh[...], fl[...], gh[:, cols], gl[:, cols])
            new = jnp.maximum(ff[:, cols] + (pp[:, cols] - fg) * inv[k], floor_value)
            ff[:, cols] = new
            hi, lo = split(new)
            fh[:, cols] = hi
            fl[:, cols] = lo
    n = n // len(outs)
    for k, out in enumerate(outs):
        out[...] = ff[n * k : n * (k + 1), :]


def sweep(product, start, axis, rows, pieces, nout):
    return pl.pallas_call(
        functools.partial(sweep_kernel, axis),
        out_shape=[sds(rows // nout, 512)] * nout,
        in_specs=[VM, HBM, VM, VM],
        out_specs=[VM] * nout,
        scratch_shapes=[
            pltpu.VMEM((512, 512), f32),
            pltpu.VMEM((512, 512), bf16),
            pltpu.VMEM((512, 512), bf16),
            pltpu.VMEM((rows, 512), bf16),
            pltpu.VMEM((rows, 512), bf16),
            pltpu.VMEM((rows, 512), f32),
            pltpu.VMEM((rows, 512), f32),
            pltpu.SemaphoreType.DMA,
        ],
        compiler_params=params(50),
        cost_estimate=cost(72 * rows * 512 * 512, 4 << 20),
        name="sweep",
    )(product, start, *pieces)


def lay_h_kernel(*refs):
    ins, out = refs[:8], refs[8]
    z, y, _, _ = place()
    for half in range(2):
        for j in range(4):
            for i in range(4):
                dz, dy = (REL[i], REL[j]) if half == 0 else (REL[j], REL[i])
                row = pl.multiple_of(64 * (4 * ((z + dz) % 4) + (y + dy) % 4) + 32 * half, 32)
                out[pl.ds(row, 32), :] = ins[4 * half + j][32 * i : 32 * (i + 1), :]


def lay_h(pieces):
    return pl.pallas_call(
        lay_h_kernel,
        out_shape=sds(1024, 512),
        in_specs=[VM] * 8,
        out_specs=VM,
        compiler_params=params(6),
        cost_estimate=cost(0, 4 << 20),
        name="lay_h",
    )(*pieces)


def moves(axis, dim):
    out = {}
    for r in range(4):
        pairs = []
        if axis == "col":
            for i in range(8):
                x, c = i // 2, i % 2
                pairs.append((i, 2 * x + 1 - c) if dim == "core" else (i, 2 * ((x + r) % 4) + c))
        else:
            for i in range(16):
                z, y = i // 4, i % 4
                pairs.append((i, 4 * ((z + r) % 4) + y) if dim == "z" else (i, 4 * z + (y + r) % 4))
        out[r] = pairs
    return out


XGROUPS = [[0, 2, 4, 6], [1, 3, 5, 7]]
CORE, X = moves("col", "core"), moves("col", "x")
Y, Z = moves("samp", "y"), moves("samp", "z")


def swap(a):
    return lax.ppermute(a, "col", CORE[0])


def send(a, axis, table, r):
    return lax.ppermute(a, axis, table[r])


def fetch(a, axis, table):
    return [lax.ppermute(a, axis, table[(4 - r) % 4]) for r in REL[1:]]


def after(a, *others):
    return lax.optimization_barrier((a,) + others)[0]


def join_kernel(nout, *refs):
    ins, outs = refs[:-nout], refs[-nout:]
    n = len(ins) // nout
    for k, out in enumerate(outs):
        rows = ins[n * k].shape[0]
        for i in range(n):
            out[rows * i : rows * (i + 1), :] = ins[n * k + i][...]


def join(parts, nout=1):
    rows = parts[0].shape[0] * len(parts) // nout
    out = pl.pallas_call(
        functools.partial(join_kernel, nout),
        out_shape=[sds(rows, 512)] * nout,
        in_specs=[VM] * len(parts),
        out_specs=[VM] * nout,
        compiler_params=params(4),
        cost_estimate=cost(0, rows * nout * 4096),
        name="join",
    )(*parts)
    return out if nout > 1 else out[0]


def add_kernel(n, *refs):
    total = refs[0][...]
    for r in refs[1:n]:
        total = total + r[...]
    refs[-1][...] = total


def add(parts):
    rows = parts[0].shape[0]
    return pl.pallas_call(
        functools.partial(add_kernel, len(parts)),
        out_shape=sds(rows, 512),
        in_specs=[VM] * len(parts),
        out_specs=VM,
        compiler_params=params(4),
        cost_estimate=cost(rows * 512 * len(parts), rows * 4096 * len(parts)),
        name="add",
    )(*parts)


def deal(pieces, axis, table):
    return [pieces[0]] + [send(pieces[k], axis, table, REL[k]) for k in (1, 2, 3)]


def spread(strip):
    strip = join([strip] + fetch(strip, "samp", Z))
    return join([strip] + fetch(strip, "samp", Y))


def shards(spectra, w_start, h_start):
    g_mine, g_theirs = gram_h(h_start, spectra)
    strip = add([g_mine, swap(g_theirs)])

    a1, hh, hl = prod(spectra, after(h_start, strip), (0, 1), True)
    r1 = swap(a1)
    strip = add([after(strip, a1)] + fetch(strip, "col", X))
    h = (after(hh, strip), hl)
    a2 = prod(spectra, h, (2, 3), True)
    r2 = swap(a2)
    low = prod(spectra, h, (0, 1), False, after(r1, a2))
    both = prod(spectra, h, (2, 3), False, r2, low)
    product = lax.all_to_all(both, "col", 0, 0, axis_index_groups=XGROUPS, tiled=True)

    part = spread(after(strip, both))
    (w,) = sweep(product, w_start, "col", 256, (part, swap(part)), 1)

    ws = swap(w)
    slices = gram_w(w, ws)
    flipped = flip(after(spectra, slices[0]))
    slices = deal(slices, "col", X)
    part = add([after(slices[0], *flipped)] + slices[1:])
    late = after(w, *flipped)
    near_p, near_m, far = send(late, "col", X, 3), send(late, "col", X, 1), send(late, "col", X, 2)
    carry = back(flipped, (w, after(ws, part)), ((0, False), (0, True)))
    part = add([after(part, carry[0])] + fetch(part, "samp", Y))
    near_p, near_m = after(near_p, part), after(near_m, part)
    sib_p, sib_m = swap(near_p), swap(near_m)
    carry = back(flipped, (near_p, near_m), ((1, False), (3, False)), carry)
    part = add([after(part, carry[0])] + fetch(part, "samp", Z))
    carry = back(flipped, (sib_p, sib_m), ((1, True), (3, True)), carry)
    sib_f = swap(after(far, part))
    carry = (after(carry[0], part), carry[1])
    back_sum, w_out = back(flipped, (far, sib_f), ((2, False), (2, True)), carry, True)

    product = lax.all_to_all(back_sum, "samp", 0, 0, tiled=True)
    part = after(part, back_sum)
    part = join([part] + fetch(part, "col", X))
    ha, hb = sweep(product, h_start, "samp", 64, (part, swap(part)), 2)

    row_a, row_b = join([ha] + fetch(ha, "samp", Z) + [hb] + fetch(hb, "samp", Y), 2)
    h_out = lay_h([row_a] + fetch(row_a, "samp", Y) + [row_b] + fetch(row_b, "samp", Z))
    return (w_out, h_out)


def solution(mesh):
    return jax.shard_map(
        shards,
        mesh=mesh,
        in_specs=(P("samp", "col"), P("samp", None), P("col", None)),
        out_specs=(P("samp", None), P("col", None)),
        check_vma=False,
    )
```
